256 devices in a mesh: shard: 16 (over y, z_hi, core), rep: 16 (over x, z_lo).
Axes of the slice: x: 4, y: 4, z: 8 (z_hi: 2, z_lo: 4; z = z_hi * 4 + z_lo), core: 2. Of those that a mesh axis runs over, the one named last changes fastest.
Arguments:
- inputs: bfloat16 [50432, 768], P(('shard', 'rep')), may hold values from -6 to 6
- norm1_gain: float32 [768], replicated, may hold values from 0.25 to 1.75
- w_qkv: bfloat16 [768, 2304], P('shard'), may hold values from -0.21875 to 0.21875
- w_proj: bfloat16 [768, 768], P('shard'), may hold values from -0.875 to 0.875
- norm2_gain: float32 [768], replicated, may hold values from 0.25 to 1.75
- w_router: bfloat16 [768, 32], P('shard'), may hold values from -0.21875 to 0.21875
- w_expert_in: bfloat16 [2, 768, 3072], P(None, 'shard'), may hold values from -0.21875 to 0.21875
- w_expert_out: bfloat16 [2, 3072, 768], P(None, 'shard'), may hold values from -0.875 to 0.875
- expert_ids: int32 [50432, 2], P(('shard', 'rep')), may hold values from 0 to 1, all different within a row
- capacity: int32 [2], replicated, may hold values from 64 to 128, as said below
- cotangent: bfloat16 [50432, 768], P(('shard', 'rep')), may hold values from -6 to 6
Outputs:
- outputs: bfloat16 [50432, 768], P(('shard', 'rep'))
- grad_inputs: float32 [50432, 768], P(('shard', 'rep'))
- grad_norm1_gain: float32 [768], replicated
- grad_qkv: float32 [768, 2304], P('shard')
- grad_proj: float32 [768, 768], P('shard')
- grad_norm2_gain: float32 [768], replicated
- grad_router: float32 [768, 32], P('shard')
- grad_expert_in: float32 [2, 768, 3072], P(None, 'shard')
- grad_expert_out: float32 [2, 3072, 768], P(None, 'shard')
The draws below stay inside these ranges and needn't reach their ends.
Inputs may be any that keep to these rules, and one draw needn't show every extreme that they name: Every expert's capacity is 64 to 128; some expert has exactly 128. `expert_ids`: the two experts of a token differ.
All inputs are finite; a program needn't handle non-finite values.
Results may differ from the reference program's by a relative error of at most 0.025.
Values may be sent and summed in bfloat16 or wider, within the bound.
No kernel may reach another device: no remote copies, remote signals or barrier semaphores. Data moves between devices by JAX's collectives and lax.ppermute only.
A program may use at most 128 MiB of HBM per device.

```python
import jax
import jax.numpy as jnp
from jax import lax

D = 768
HEADS = 12
HD = 64
HID = 3072
EXPERTS = 32
E_WIN = 2
SEQ = 197
IMG_DEV = 1
TOK_DEV = 197
CAP = 128
TOKENS = 50432


def draw_capacity(key, part):
    lower = jax.random.randint(jax.random.fold_in(key, 11), (E_WIN,), CAP // 2, CAP + 1)
    which = jax.random.randint(jax.random.fold_in(key, 12), (), 0, E_WIN)
    return jnp.where(jnp.arange(E_WIN) == which, CAP, lower).astype(jnp.int32)


def level_of(rng, dims, cuts, low, high):
    level = 1.0
    for dim, parts in cuts:
        heights = jax.random.uniform(jax.random.fold_in(jax.random.fold_in(rng, 6), dim), (parts,), jnp.float32, low / len(cuts), high / len(cuts))
        level = level * jnp.repeat(jnp.exp(heights), dims[dim] // parts).reshape((-1,) + (1,) * (len(dims) - 1 - dim))
    return level


def different_ones(own_key, rows, count, top, lift):
    order = jax.random.permutation(jax.random.fold_in(own_key, 1), count)
    pull = order
    for power in range(3):
        pull = pull * pull // count
    pull = pull * lift // count
    lots = jax.random.randint(jax.random.fold_in(own_key, 2), (rows, count), 0, 4096) + pull
    sure = jax.random.permutation(jax.random.fold_in(own_key, 3), rows)[jnp.arange(count) % rows]
    lots = jnp.where(jnp.arange(rows)[:, None] == sure[None, :], 1 << 14, lots)
    merit = lots * count + jnp.arange(count)
    return lax.top_k(merit.astype(jnp.int32), top)[1].astype(jnp.int32)


def bell_draw(own_key, dims, scale, reach, split=(), kind=jnp.bfloat16):
    entries = scale * jax.random.normal(own_key, dims, jnp.float32)
    if split:
        entries = entries * level_of(own_key, dims, split, -0.22, 0.18)
    return jnp.clip(entries, -reach, reach).astype(kind)


def setup_inputs(seed: int = 0) -> dict:
    arg_keys = jax.random.split(jax.random.key(seed), 12)
    inputs = bell_draw(arg_keys[0], (TOKENS, D), 1.0, 6.0, ((0, 256),))
    norm1_gain = jnp.clip(1.0 + 0.15 * jax.random.normal(arg_keys[1], (D,), jnp.float32), 0.25, 1.75)
    w_qkv = bell_draw(arg_keys[2], (D, 3 * D), D ** -0.5, 0.21875, ((0, 16),))
    w_proj = bell_draw(arg_keys[3], (D, D), (D // 16) ** -0.5, 0.875, ((0, 16),))
    norm2_gain = jnp.clip(1.0 + 0.15 * jax.random.normal(arg_keys[4], (D,), jnp.float32), 0.25, 1.75)
    w_router = bell_draw(arg_keys[5], (D, EXPERTS), D ** -0.5, 0.21875, ((0, 16),))
    w_expert_in = bell_draw(arg_keys[6], (E_WIN, D, HID), D ** -0.5, 0.21875, ((1, 16),))
    w_expert_out = bell_draw(arg_keys[7], (E_WIN, HID, D), (HID // 64) ** -0.5, 0.875, ((1, 16),))
    expert_ids = different_ones(arg_keys[8], TOKENS, E_WIN, 2, 0)
    capacity = draw_capacity(jax.random.fold_in(arg_keys[11], 71), 0)
    cotangent = bell_draw(arg_keys[10], (TOKENS, D), 1.0, 6.0, ((0, 256),))
    return dict(inputs=inputs, norm1_gain=norm1_gain, w_qkv=w_qkv, w_proj=w_proj, norm2_gain=norm2_gain, w_router=w_router, w_expert_in=w_expert_in, w_expert_out=w_expert_out, expert_ids=expert_ids, capacity=capacity, cotangent=cotangent)


EPS = 1e-06

def layer_norm(values, gain):
    centred = values - lax.optimization_barrier(jnp.mean(values, axis=-1, keepdims=True))
    inverse = lax.rsqrt(lax.optimization_barrier(jnp.mean(centred * centred, axis=-1, keepdims=True)) + EPS)
    normed = centred * inverse
    return (normed, inverse, (normed * gain).astype(jnp.bfloat16))

def layer_norm_back(grad_out, normed, inverse, gain):
    scaled = grad_out * gain
    grad_in = inverse * (scaled - lax.optimization_barrier(jnp.mean(scaled, axis=-1, keepdims=True)) - normed * lax.optimization_barrier(jnp.mean(scaled * normed, axis=-1, keepdims=True)))
    return (grad_in, lax.optimization_barrier(jnp.sum(grad_out * normed, axis=0)))

def heads_view(block, images):
    return block.reshape(images, SEQ, HEADS, HD).astype(jnp.float32)

def rounded(values):
    return lax.optimization_barrier(values.astype(jnp.bfloat16)).astype(jnp.float32)

def attention_scores(qkv, images):
    width = HEADS * HD
    query = heads_view(qkv[:, :width], images)
    keys = heads_view(qkv[:, width:2 * width], images)
    values = heads_view(qkv[:, 2 * width:], images)
    scores = jnp.einsum('bqhd,bkhd->bhqk', query, keys) * HD ** (-0.5)
    return (query, keys, values, scores)

def attention_forward(qkv, images):
    query, keys, values, scores = attention_scores(qkv, images)
    logsum = jax.nn.logsumexp(scores, axis=-1, keepdims=True)
    probs = rounded(jnp.exp(scores - logsum))
    mixed = jnp.einsum('bhqk,bkhd->bqhd', probs, values).astype(jnp.bfloat16)
    return (mixed.reshape(images * SEQ, HEADS * HD), logsum)

def attention_backward(qkv, mixed, logsum, grad_mixed, images):
    query, keys, values, scores = attention_scores(qkv, images)
    probs_full = jnp.exp(scores - logsum)
    probs = rounded(probs_full)
    grad_out = heads_view(grad_mixed, images)
    out_rows = heads_view(mixed, images)
    grad_values = jnp.einsum('bhqk,bqhd->bkhd', probs, grad_out)
    grad_probs = jnp.einsum('bqhd,bkhd->bhqk', grad_out, values)
    delta = jnp.transpose(lax.optimization_barrier(jnp.sum(grad_out * out_rows, axis=-1)), (0, 2, 1))[..., None]
    grad_scores = rounded(probs_full * (grad_probs - delta))
    scale = HD ** (-0.5)
    grad_query = jnp.einsum('bhqk,bkhd->bqhd', grad_scores, keys) * scale
    grad_keys = jnp.einsum('bhqk,bqhd->bkhd', grad_scores, query) * scale
    width = HEADS * HD
    rows = images * SEQ
    return jnp.concatenate([grad_query.reshape(rows, width), grad_keys.reshape(rows, width), grad_values.reshape(rows, width)], axis=1).astype(jnp.bfloat16)

def route_masks(expert_ids, capacity):
    count = expert_ids.shape[0]
    picked_hot = (expert_ids[:, :, None] == jnp.arange(E_WIN)[None, None, :]).astype(jnp.int32)
    ordered = jnp.transpose(picked_hot, (1, 0, 2)).reshape(2 * count, E_WIN)
    before = jnp.cumsum(ordered, axis=0) - ordered
    position = lax.optimization_barrier(jnp.sum(before * ordered, axis=1)).reshape(2, count).T
    limit = lax.optimization_barrier(jnp.sum(picked_hot * capacity[None, None, :], axis=2))
    kept_mask = (position < limit).astype(jnp.float32)
    slot_hot = (position[:, :, None] == jnp.arange(CAP)[None, None, :]).astype(jnp.float32)
    return kept_mask[:, :, None, None] * picked_hot.astype(jnp.float32)[:, :, :, None] * slot_hot[:, :, None, :]

def reference(inputs, norm1_gain, w_qkv, w_proj, norm2_gain, w_router, w_expert_in, w_expert_out, expert_ids, capacity, cotangent):
    blocks = inputs.shape[0] // TOK_DEV
    high = lax.Precision.HIGHEST
    wide_in = w_expert_in.astype(jnp.float32)
    wide_out = w_expert_out.astype(jnp.float32)

    def one_block(carry, stacked):
        sum_g1, sum_qkv, sum_proj, sum_g2, sum_router, sum_in, sum_out = carry
        x_rows, route_ids, grad_rows_out = stacked
        x_float = x_rows.astype(jnp.float32)
        normed1, inverse1, hidden1 = layer_norm(x_float, norm1_gain)
        qkv = jnp.dot(hidden1, w_qkv, preferred_element_type=jnp.float32).astype(jnp.bfloat16)
        mixed, logsum = attention_forward(qkv, IMG_DEV)
        attended = x_float + jnp.dot(mixed, w_proj, preferred_element_type=jnp.float32)
        normed2, inverse2, hidden2 = layer_norm(attended, norm2_gain)
        logits = jnp.dot(hidden2, w_router, preferred_element_type=jnp.float32)
        router = jax.nn.softmax(logits, axis=-1)
        expert_hot = (route_ids[:, :, None] == jnp.arange(EXPERTS)[None, None, :]).astype(jnp.float32)
        gate = lax.optimization_barrier(jnp.sum(router[:, None, :] * expert_hot, axis=2))
        masks = route_masks(route_ids, capacity)
        dispatch = lax.optimization_barrier(jnp.sum(masks, axis=1))
        combine = lax.optimization_barrier(jnp.sum(masks * gate[:, :, None, None], axis=1))
        expert_rows = jnp.einsum('rec,rd->ecd', dispatch, hidden2.astype(jnp.float32)).astype(jnp.bfloat16)
        pre = jnp.einsum('ecd,edh->ech', expert_rows.astype(jnp.float32), wide_in)
        activated = jax.nn.gelu(pre, approximate=False).astype(jnp.bfloat16)
        expert_out = jnp.einsum('ech,ehd->ecd', activated.astype(jnp.float32), wide_out).astype(jnp.bfloat16)
        eout_float = expert_out.astype(jnp.float32)
        moe = jnp.einsum('rec,ecd->rd', combine, eout_float, precision=high)
        outputs = (attended + moe).astype(jnp.bfloat16)
        grad = grad_rows_out.astype(jnp.float32)
        matched = jnp.einsum('rd,ecd->rec', grad, eout_float, precision=high)
        grad_gate = lax.optimization_barrier(jnp.sum(masks * matched[:, None, :, :], axis=(2, 3)))
        grad_eout = jnp.einsum('rec,rd->ecd', combine, grad, precision=high).astype(jnp.bfloat16)
        grad_act = jnp.einsum('ecd,ehd->ech', grad_eout.astype(jnp.float32), wide_out)
        slope = 0.5 * (1.0 + jax.scipy.special.erf(pre * 0.7071067811865476)) + pre * jnp.exp(-0.5 * pre * pre) * 0.3989422804014327
        grad_pre = (grad_act * slope).astype(jnp.bfloat16)
        sum_out = sum_out + jnp.einsum('ech,ecd->ehd', activated.astype(jnp.float32), grad_eout.astype(jnp.float32))
        sum_in = sum_in + jnp.einsum('ecd,ech->edh', expert_rows.astype(jnp.float32), grad_pre.astype(jnp.float32))
        grad_rows = jnp.einsum('ech,edh->ecd', grad_pre.astype(jnp.float32), wide_in).astype(jnp.bfloat16)
        grad_probs = lax.optimization_barrier(jnp.sum(grad_gate[:, :, None] * expert_hot, axis=1))
        grad_logits = (router * (grad_probs - lax.optimization_barrier(jnp.sum(router * grad_probs, axis=-1, keepdims=True)))).astype(jnp.bfloat16)
        sum_router = sum_router + jnp.dot(hidden2.T, grad_logits, preferred_element_type=jnp.float32)
        grad_hidden2 = jnp.einsum('rec,ecd->rd', dispatch, grad_rows.astype(jnp.float32)) + jnp.dot(grad_logits, w_router.T, preferred_element_type=jnp.float32)
        grad_norm2, gain2 = layer_norm_back(grad_hidden2, normed2, inverse2, norm2_gain)
        grad_attended = grad + grad_norm2
        grad_branch = grad_attended.astype(jnp.bfloat16)
        sum_proj = sum_proj + jnp.dot(mixed.T, grad_branch, preferred_element_type=jnp.float32)
        grad_mixed = jnp.dot(grad_branch, w_proj.T, preferred_element_type=jnp.float32).astype(jnp.bfloat16)
        grad_qkv_rows = attention_backward(qkv, mixed, logsum, grad_mixed, IMG_DEV)
        sum_qkv = sum_qkv + jnp.dot(hidden1.T, grad_qkv_rows, preferred_element_type=jnp.float32)
        grad_hidden1 = jnp.dot(grad_qkv_rows, w_qkv.T, preferred_element_type=jnp.float32)
        grad_norm1, gain1 = layer_norm_back(grad_hidden1, normed1, inverse1, norm1_gain)
        grad_inputs = grad_attended + grad_norm1
        carry = (sum_g1 + gain1, sum_qkv, sum_proj, sum_g2 + gain2, sum_router, sum_in, sum_out)
        return (carry, (outputs, grad_inputs))
    start = (jnp.zeros((D,), jnp.float32), jnp.zeros((D, 3 * D), jnp.float32), jnp.zeros((D, D), jnp.float32), jnp.zeros((D,), jnp.float32), jnp.zeros((D, EXPERTS), jnp.float32), jnp.zeros((E_WIN, D, HID), jnp.float32), jnp.zeros((E_WIN, HID, D), jnp.float32))
    stacked = (inputs.reshape(blocks, TOK_DEV, D), expert_ids.reshape(blocks, TOK_DEV, 2), cotangent.reshape(blocks, TOK_DEV, D))
    carry, (outputs, grad_inputs) = lax.scan(one_block, start, stacked)
    sum_g1, sum_qkv, sum_proj, sum_g2, sum_router, sum_in, sum_out = carry
    return (outputs.reshape(blocks * TOK_DEV, D), grad_inputs.reshape(blocks * TOK_DEV, D), sum_g1, sum_qkv, sum_proj, sum_g2, sum_router, sum_in, sum_out)
```

```python
import jax
import jax.numpy as jnp
from jax import lax
from jax.sharding import PartitionSpec as P

HEADS = 12
HD = 64
EXPERTS = 32
E_WIN = 2
SEQ = 197
CAP = 128


EPS = 1e-06


def layer_norm(values, gain):
    centred = values - jnp.mean(values, axis=-1, keepdims=True)
    inverse = lax.rsqrt(jnp.mean(centred * centred, axis=-1, keepdims=True) + EPS)
    normed = centred * inverse
    return (normed, inverse, (normed * gain).astype(jnp.bfloat16))


def layer_norm_back(grad_out, normed, inverse, gain):
    scaled = grad_out * gain
    grad_in = inverse * (
        scaled
        - jnp.mean(scaled, axis=-1, keepdims=True)
        - normed * jnp.mean(scaled * normed, axis=-1, keepdims=True)
    )
    return (grad_in, jnp.sum(grad_out * normed, axis=0))


def butterfly_sum(value, axis, size, wire=None):
    step = 1
    while step < size:
        pairs = [(i, i ^ step) for i in range(size)]
        sent = value if wire is None else value.astype(wire)
        other = lax.ppermute(sent, axis, pairs)
        value = sent.astype(jnp.float32) + other.astype(jnp.float32)
        step *= 2
    return value


def heads_view(block, images):
    return block.reshape(images, SEQ, HEADS, HD)


def attention_scores(qkv, images):
    width = HEADS * HD
    query = heads_view(qkv[:, :width], images)
    keys = heads_view(qkv[:, width : 2 * width], images)
    values = heads_view(qkv[:, 2 * width :], images)
    scores = jnp.einsum(
        "bqhd,bkhd->bhqk", query, keys, preferred_element_type=jnp.float32
    ) * HD ** (-0.5)
    return (query, keys, values, scores)


def attention_forward(qkv, images):
    query, keys, values, scores = attention_scores(qkv, images)
    logsum = jax.nn.logsumexp(scores, axis=-1, keepdims=True)
    probs = jnp.exp(scores - logsum).astype(jnp.bfloat16)
    mixed = jnp.einsum("bhqk,bkhd->bqhd", probs, values, preferred_element_type=jnp.float32).astype(
        jnp.bfloat16
    )
    return (mixed.reshape(images * SEQ, HEADS * HD), logsum)


def attention_backward(qkv, mixed, logsum, grad_mixed, images):
    query, keys, values, scores = attention_scores(qkv, images)
    probs_full = jnp.exp(scores - logsum)
    probs = probs_full.astype(jnp.bfloat16)
    grad_out = heads_view(grad_mixed, images)
    out_rows = heads_view(mixed, images)
    grad_values = jnp.einsum("bhqk,bqhd->bkhd", probs, grad_out, preferred_element_type=jnp.float32)
    grad_probs = jnp.einsum("bqhd,bkhd->bhqk", grad_out, values, preferred_element_type=jnp.float32)
    delta = jnp.sum(grad_out.astype(jnp.float32) * out_rows.astype(jnp.float32), axis=-1)
    delta = jnp.transpose(delta, (0, 2, 1))[..., None]
    grad_scores = (probs_full * (grad_probs - delta)).astype(jnp.bfloat16)
    scale = HD ** (-0.5)
    grad_query = (
        jnp.einsum("bhqk,bkhd->bqhd", grad_scores, keys, preferred_element_type=jnp.float32) * scale
    )
    grad_keys = (
        jnp.einsum("bhqk,bqhd->bkhd", grad_scores, query, preferred_element_type=jnp.float32)
        * scale
    )
    width = HEADS * HD
    rows = images * SEQ
    return jnp.concatenate(
        [
            grad_query.reshape(rows, width),
            grad_keys.reshape(rows, width),
            grad_values.reshape(rows, width),
        ],
        axis=1,
    ).astype(jnp.bfloat16)


def route_masks(expert_ids, capacity):
    count = expert_ids.shape[0]
    picked_hot = (expert_ids[:, :, None] == jnp.arange(E_WIN)[None, None, :]).astype(jnp.int32)
    ordered = jnp.transpose(picked_hot, (1, 0, 2)).reshape(2 * count, E_WIN)
    before = jnp.cumsum(ordered, axis=0) - ordered
    position = jnp.sum(before * ordered, axis=1).reshape(2, count).T
    limit = jnp.sum(picked_hot * capacity[None, None, :], axis=2)
    kept_mask = (position < limit).astype(jnp.float32)
    slot_hot = (position[:, :, None] == jnp.arange(CAP)[None, None, :]).astype(jnp.float32)
    return (
        kept_mask[:, :, None, None]
        * picked_hot.astype(jnp.float32)[:, :, :, None]
        * slot_hot[:, :, None, :]
    )


def body(
    inputs,
    norm1_gain,
    w_qkv,
    w_proj,
    norm2_gain,
    w_router,
    w_expert_in,
    w_expert_out,
    expert_ids,
    capacity,
    cotangent,
):
    high = lax.Precision.HIGHEST
    images = inputs.shape[0] // SEQ
    shard_rows = w_qkv.shape[0]
    hid_rows = w_expert_out.shape[1]
    width = HEADS * HD
    dense_all = lax.all_gather(
        jnp.concatenate([w_qkv, w_proj, w_router], axis=1), "shard", axis=0, tiled=True
    )
    full_qkv, full_proj, full_router = (
        dense_all[:, : 3 * width],
        dense_all[:, 3 * width : 4 * width],
        dense_all[:, 4 * width :],
    )
    x_float = inputs.astype(jnp.float32)
    normed1, inverse1, hidden1 = layer_norm(x_float, norm1_gain)
    qkv = jnp.dot(hidden1, full_qkv, preferred_element_type=jnp.float32).astype(jnp.bfloat16)
    mixed, logsum = attention_forward(qkv, images)
    attended = x_float + jnp.dot(mixed, full_proj, preferred_element_type=jnp.float32)
    normed2, inverse2, hidden2 = layer_norm(attended, norm2_gain)
    logits = jnp.dot(hidden2, full_router, preferred_element_type=jnp.float32)
    router = jax.nn.softmax(logits, axis=-1)
    expert_hot = (expert_ids[:, :, None] == jnp.arange(EXPERTS)[None, None, :]).astype(jnp.float32)
    gate = jnp.sum(router[:, None, :] * expert_hot, axis=2)
    masks = route_masks(expert_ids, capacity)
    dispatch_float = jnp.sum(masks, axis=1)
    dispatch = dispatch_float.astype(jnp.bfloat16)
    combine = jnp.sum(masks * gate[:, :, None, None], axis=1)
    expert_rows = jnp.einsum(
        "rec,rd->ecd", dispatch, hidden2, preferred_element_type=jnp.float32
    ).astype(jnp.bfloat16)
    kept_weights = []
    pre_list = []
    activated_list = []
    eout_list = []
    for expert in range(E_WIN):
        first, second = (
            lax.all_gather(w_expert_in[expert], "shard", axis=0, tiled=True),
            lax.all_gather(w_expert_out[expert], "shard", axis=0, tiled=True),
        )
        kept_weights.append((first, second))
        pre = jnp.dot(expert_rows[expert], first, preferred_element_type=jnp.float32)
        activated = jax.nn.gelu(pre, approximate=False).astype(jnp.bfloat16)
        pre_list.append(pre)
        activated_list.append(activated)
        eout_list.append(
            jnp.dot(activated, second, preferred_element_type=jnp.float32).astype(jnp.bfloat16)
        )
    expert_out = jnp.stack(eout_list)
    eout_float = expert_out.astype(jnp.float32)
    moe = jnp.einsum("rec,ecd->rd", combine, eout_float, precision=high)
    outputs = (attended + moe).astype(jnp.bfloat16)
    grad = cotangent.astype(jnp.float32)
    matched = jnp.einsum("rd,ecd->rec", grad, eout_float, precision=high)
    grad_gate = jnp.sum(masks * matched[:, None, :, :], axis=(2, 3))
    grad_eout = jnp.einsum("rec,rd->ecd", combine, grad, precision=high).astype(jnp.bfloat16)
    back_qkv, back_proj, back_router = (full_qkv, full_proj, full_router)
    in_list = []
    out_list = []
    grad_rows_list = []
    for expert in range(E_WIN):
        first, second = kept_weights[expert]
        pre = pre_list[expert]
        grad_act = jnp.einsum(
            "cd,hd->ch", grad_eout[expert], second, preferred_element_type=jnp.float32
        )
        slope = (
            0.5 * (1.0 + jax.scipy.special.erf(pre * 0.7071067811865476))
            + pre * jnp.exp(-0.5 * pre * pre) * 0.3989422804014327
        )
        grad_pre = (grad_act * slope).astype(jnp.bfloat16)
        grad_rows_list.append(
            jnp.einsum("ch,dh->cd", grad_pre, first, preferred_element_type=jnp.float32).astype(
                jnp.bfloat16
            )
        )
        rows_here = expert_rows[expert]
        act_here = activated_list[expert]
        eout_here = grad_eout[expert]

        def in_term(start, count, rows_here=rows_here, grad_pre=grad_pre):
            return jnp.einsum("cd,ch->dh", rows_here, grad_pre, preferred_element_type=jnp.float32)

        def out_term(start, count, act_here=act_here, eout_here=eout_here):
            return jnp.einsum("ch,cd->hd", act_here, eout_here, preferred_element_type=jnp.float32)

        in_list.append(
            lax.psum_scatter(
                in_term(jnp.int32(0), shard_rows * lax.axis_size("shard")).astype(jnp.bfloat16),
                "shard",
                scatter_dimension=0,
                tiled=True,
            )
        )
        out_list.append(
            lax.psum_scatter(
                out_term(jnp.int32(0), hid_rows * lax.axis_size("shard")).astype(jnp.bfloat16),
                "shard",
                scatter_dimension=0,
                tiled=True,
            )
        )
    grad_rows = jnp.stack(grad_rows_list)
    grad_probs = jnp.sum(grad_gate[:, :, None] * expert_hot, axis=1)
    grad_logits = (
        router * (grad_probs - jnp.sum(router * grad_probs, axis=-1, keepdims=True))
    ).astype(jnp.bfloat16)
    grad_hidden2 = jnp.einsum(
        "rec,ecd->rd", dispatch, grad_rows, preferred_element_type=jnp.float32
    ) + jnp.einsum("re,de->rd", grad_logits, back_router, preferred_element_type=jnp.float32)
    grad_norm2, gain2 = layer_norm_back(grad_hidden2, normed2, inverse2, norm2_gain)
    grad_attended = grad + grad_norm2
    grad_branch = grad_attended.astype(jnp.bfloat16)
    grad_mixed = jnp.einsum(
        "rk,dk->rd", grad_branch, back_proj, preferred_element_type=jnp.float32
    ).astype(jnp.bfloat16)
    grad_qkv_rows = attention_backward(qkv, mixed, logsum, grad_mixed, images)
    grad_hidden1 = jnp.einsum(
        "rk,dk->rd", grad_qkv_rows, back_qkv, preferred_element_type=jnp.float32
    )
    grad_norm1, gain1 = layer_norm_back(grad_hidden1, normed1, inverse1, norm1_gain)
    grad_inputs = grad_attended + grad_norm1
    n_shard = lax.axis_size("shard")
    n_rep = lax.axis_size("rep")
    gains = butterfly_sum(jnp.stack([gain1, gain2]), "shard", n_shard)
    gains = butterfly_sum(gains, "rep", n_rep)
    gain1_total, gain2_total = gains[0], gains[1]
    dense_local = lax.psum_scatter(
        jnp.concatenate(
            [
                jnp.einsum("rc,rk->ck", hidden1, grad_qkv_rows, preferred_element_type=jnp.float32),
                jnp.einsum("rc,rk->ck", mixed, grad_branch, preferred_element_type=jnp.float32),
                jnp.einsum("rc,rk->ck", hidden2, grad_logits, preferred_element_type=jnp.float32),
            ],
            axis=1,
        ).astype(jnp.bfloat16),
        "shard",
        scatter_dimension=0,
        tiled=True,
    )
    dense_total, in_total, out_total = (
        butterfly_sum(dense_local, "rep", n_rep, jnp.bfloat16),
        butterfly_sum(jnp.stack(in_list), "rep", n_rep, jnp.bfloat16),
        butterfly_sum(jnp.stack(out_list), "rep", n_rep, jnp.bfloat16),
    )
    return (
        outputs,
        grad_inputs,
        gain1_total,
        dense_total[:, : 3 * width],
        dense_total[:, 3 * width : 4 * width],
        gain2_total,
        dense_total[:, 4 * width :],
        in_total,
        out_total,
    )


def solution(mesh):
    in_specs = (
        P(("shard", "rep"), None),
        P(),
        P("shard", None),
        P("shard", None),
        P(),
        P("shard", None),
        P(None, "shard", None),
        P(None, "shard", None),
        P(("shard", "rep"), None),
        P(),
        P(("shard", "rep"), None),
    )
    out_specs = (
        P(("shard", "rep"), None),
        P(("shard", "rep"), None),
        P(),
        P("shard", None),
        P("shard", None),
        P(),
        P("shard", None),
        P(None, "shard", None),
        P(None, "shard", None),
    )
    return jax.shard_map(body, mesh=mesh, in_specs=in_specs, out_specs=out_specs, check_vma=False)
```

```python
import jax
import jax.numpy as jnp
from jax import lax
from jax.sharding import PartitionSpec as P

HEADS = 12
HD = 64
EXPERTS = 32
E_WIN = 2
SEQ = 197
CAP = 128


EPS = 1e-06


def layer_norm(values, gain):
    centred = values - jnp.mean(values, axis=-1, keepdims=True)
    inverse = lax.rsqrt(jnp.mean(centred * centred, axis=-1, keepdims=True) + EPS)
    normed = centred * inverse
    return (normed, inverse, (normed * gain).astype(jnp.bfloat16))


def layer_norm_back(grad_out, normed, inverse, gain):
    scaled = grad_out * gain
    grad_in = inverse * (
        scaled
        - jnp.mean(scaled, axis=-1, keepdims=True)
        - normed * jnp.mean(scaled * normed, axis=-1, keepdims=True)
    )
    return (grad_in, jnp.sum(grad_out * normed, axis=0))


def butterfly_sum(value, axis, size, wire=None):
    step = 1
    while step < size:
        pairs = [(i, i ^ step) for i in range(size)]
        sent = value if wire is None else value.astype(wire)
        other = lax.ppermute(sent, axis, pairs)
        value = sent.astype(jnp.float32) + other.astype(jnp.float32)
        step *= 2
    return value


def heads_view(block, images):
    return block.reshape(images, SEQ, HEADS, HD)


def attention_scores(qkv, images):
    width = HEADS * HD
    query = heads_view(qkv[:, :width], images)
    keys = heads_view(qkv[:, width : 2 * width], images)
    values = heads_view(qkv[:, 2 * width :], images)
    scores = jnp.einsum(
        "bqhd,bkhd->bhqk", query, keys, preferred_element_type=jnp.float32
    ) * HD ** (-0.5)
    return (query, keys, values, scores)


def attention_forward(qkv, images):
    query, keys, values, scores = attention_scores(qkv, images)
    logsum = jax.nn.logsumexp(scores, axis=-1, keepdims=True)
    probs = jnp.exp(scores - logsum).astype(jnp.bfloat16)
    mixed = jnp.einsum("bhqk,bkhd->bqhd", probs, values, preferred_element_type=jnp.float32).astype(
        jnp.bfloat16
    )
    return (mixed.reshape(images * SEQ, HEADS * HD), logsum)


def attention_backward(qkv, mixed, logsum, grad_mixed, images):
    query, keys, values, scores = attention_scores(qkv, images)
    probs_full = jnp.exp(scores - logsum)
    probs = probs_full.astype(jnp.bfloat16)
    grad_out = heads_view(grad_mixed, images)
    out_rows = heads_view(mixed, images)
    grad_values = jnp.einsum("bhqk,bqhd->bkhd", probs, grad_out, preferred_element_type=jnp.float32)
    grad_probs = jnp.einsum("bqhd,bkhd->bhqk", grad_out, values, preferred_element_type=jnp.float32)
    delta = jnp.sum(grad_out.astype(jnp.float32) * out_rows.astype(jnp.float32), axis=-1)
    delta = jnp.transpose(delta, (0, 2, 1))[..., None]
    grad_scores = (probs_full * (grad_probs - delta)).astype(jnp.bfloat16)
    scale = HD ** (-0.5)
    grad_query = (
        jnp.einsum("bhqk,bkhd->bqhd", grad_scores, keys, preferred_element_type=jnp.float32) * scale
    )
    grad_keys = (
        jnp.einsum("bhqk,bqhd->bkhd", grad_scores, query, preferred_element_type=jnp.float32)
        * scale
    )
    width = HEADS * HD
    rows = images * SEQ
    return jnp.concatenate(
        [
            grad_query.reshape(rows, width),
            grad_keys.reshape(rows, width),
            grad_values.reshape(rows, width),
        ],
        axis=1,
    ).astype(jnp.bfloat16)


def route_masks(expert_ids, capacity):
    count = expert_ids.shape[0]
    picked_hot = (expert_ids[:, :, None] == jnp.arange(E_WIN)[None, None, :]).astype(jnp.int32)
    ordered = jnp.transpose(picked_hot, (1, 0, 2)).reshape(2 * count, E_WIN)
    before = jnp.cumsum(ordered, axis=0) - ordered
    position = jnp.sum(before * ordered, axis=1).reshape(2, count).T
    limit = jnp.sum(picked_hot * capacity[None, None, :], axis=2)
    kept_mask = (position < limit).astype(jnp.float32)
    slot_hot = (position[:, :, None] == jnp.arange(CAP)[None, None, :]).astype(jnp.float32)
    return (
        kept_mask[:, :, None, None]
        * picked_hot.astype(jnp.float32)[:, :, :, None]
        * slot_hot[:, :, None, :]
    )


def body(
    inputs,
    norm1_gain,
    w_qkv,
    w_proj,
    norm2_gain,
    w_router,
    w_expert_in,
    w_expert_out,
    expert_ids,
    capacity,
    cotangent,
):
    high = lax.Precision.HIGHEST
    images = inputs.shape[0] // SEQ
    shard_rows = w_qkv.shape[0]
    hid_rows = w_expert_out.shape[1]
    width = HEADS * HD
    dense_all = lax.all_gather(
        jnp.concatenate([w_qkv, w_proj, w_router], axis=1), "shard", axis=0, tiled=True
    )
    full_qkv, full_proj, full_router = (
        dense_all[:, : 3 * width],
        dense_all[:, 3 * width : 4 * width],
        dense_all[:, 4 * width :],
    )
    x_float = inputs.astype(jnp.float32)
    normed1, inverse1, hidden1 = layer_norm(x_float, norm1_gain)
    qkv = jnp.dot(hidden1, full_qkv, preferred_element_type=jnp.float32).astype(jnp.bfloat16)
    mixed, logsum = attention_forward(qkv, images)
    attended = x_float + jnp.dot(mixed, full_proj, preferred_element_type=jnp.float32)
    normed2, inverse2, hidden2 = layer_norm(attended, norm2_gain)
    logits = jnp.dot(hidden2, full_router, preferred_element_type=jnp.float32)
    router = jax.nn.softmax(logits, axis=-1)
    expert_hot = (expert_ids[:, :, None] == jnp.arange(EXPERTS)[None, None, :]).astype(jnp.float32)
    gate = jnp.sum(router[:, None, :] * expert_hot, axis=2)
    masks = route_masks(expert_ids, capacity)
    dispatch_float = jnp.sum(masks, axis=1)
    dispatch = dispatch_float.astype(jnp.bfloat16)
    combine = jnp.sum(masks * gate[:, :, None, None], axis=1)
    expert_rows = jnp.einsum(
        "rec,rd->ecd", dispatch, hidden2, preferred_element_type=jnp.float32
    ).astype(jnp.bfloat16)
    w_in_cols = lax.all_to_all(w_expert_in, "shard", 2, 1, tiled=True)
    rows_all = lax.all_gather(expert_rows, "shard", axis=1, tiled=True)
    pre = jnp.einsum("erd,edh->erh", rows_all, w_in_cols, preferred_element_type=jnp.float32)
    activated = jax.nn.gelu(pre, approximate=False).astype(jnp.bfloat16)
    out_part = jnp.einsum(
        "erh,ehd->erd", activated, w_expert_out, preferred_element_type=jnp.float32
    ).astype(jnp.bfloat16)
    expert_out = lax.psum_scatter(out_part, "shard", scatter_dimension=1, tiled=True)
    eout_float = expert_out.astype(jnp.float32)
    moe = jnp.einsum("rec,ecd->rd", combine, eout_float, precision=high)
    outputs = (attended + moe).astype(jnp.bfloat16)
    grad = cotangent.astype(jnp.float32)
    matched = jnp.einsum("rd,ecd->rec", grad, eout_float, precision=high)
    grad_gate = jnp.sum(masks * matched[:, None, :, :], axis=(2, 3))
    grad_eout = jnp.einsum("rec,rd->ecd", combine, grad, precision=high).astype(jnp.bfloat16)
    back_qkv, back_proj, back_router = (full_qkv, full_proj, full_router)
    geout_all = lax.all_gather(grad_eout, "shard", axis=1, tiled=True)
    grad_act = jnp.einsum(
        "erd,ehd->erh", geout_all, w_expert_out, preferred_element_type=jnp.float32
    )
    slope = (
        0.5 * (1.0 + jax.scipy.special.erf(pre * 0.7071067811865476))
        + pre * jnp.exp(-0.5 * pre * pre) * 0.3989422804014327
    )
    grad_pre = (grad_act * slope).astype(jnp.bfloat16)
    rows_part = jnp.einsum(
        "erh,edh->erd", grad_pre, w_in_cols, preferred_element_type=jnp.float32
    ).astype(jnp.bfloat16)
    grad_rows = lax.psum_scatter(rows_part, "shard", scatter_dimension=1, tiled=True)
    gin_cols = jnp.einsum("erd,erh->edh", rows_all, grad_pre, preferred_element_type=jnp.float32)
    gin_local = lax.all_to_all(gin_cols.astype(jnp.bfloat16), "shard", 1, 2, tiled=True)
    gout_local = jnp.einsum(
        "erh,erd->ehd", activated, geout_all, preferred_element_type=jnp.float32
    ).astype(jnp.bfloat16)
    grad_probs = jnp.sum(grad_gate[:, :, None] * expert_hot, axis=1)
    grad_logits = (
        router * (grad_probs - jnp.sum(router * grad_probs, axis=-1, keepdims=True))
    ).astype(jnp.bfloat16)
    grad_hidden2 = jnp.einsum(
        "rec,ecd->rd", dispatch, grad_rows, preferred_element_type=jnp.float32
    ) + jnp.einsum("re,de->rd", grad_logits, back_router, preferred_element_type=jnp.float32)
    grad_norm2, gain2 = layer_norm_back(grad_hidden2, normed2, inverse2, norm2_gain)
    grad_attended = grad + grad_norm2
    grad_branch = grad_attended.astype(jnp.bfloat16)
    grad_mixed = jnp.einsum(
        "rk,dk->rd", grad_branch, back_proj, preferred_element_type=jnp.float32
    ).astype(jnp.bfloat16)
    grad_qkv_rows = attention_backward(qkv, mixed, logsum, grad_mixed, images)
    grad_hidden1 = jnp.einsum(
        "rk,dk->rd", grad_qkv_rows, back_qkv, preferred_element_type=jnp.float32
    )
    grad_norm1, gain1 = layer_norm_back(grad_hidden1, normed1, inverse1, norm1_gain)
    grad_inputs = grad_attended + grad_norm1
    n_shard = lax.axis_size("shard")
    n_rep = lax.axis_size("rep")
    gains = butterfly_sum(jnp.stack([gain1, gain2]), "shard", n_shard)
    gains = butterfly_sum(gains, "rep", n_rep)
    gain1_total, gain2_total = gains[0], gains[1]
    dense_local = lax.psum_scatter(
        jnp.concatenate(
            [
                jnp.einsum("rc,rk->ck", hidden1, grad_qkv_rows, preferred_element_type=jnp.float32),
                jnp.einsum("rc,rk->ck", mixed, grad_branch, preferred_element_type=jnp.float32),
                jnp.einsum("rc,rk->ck", hidden2, grad_logits, preferred_element_type=jnp.float32),
            ],
            axis=1,
        ).astype(jnp.bfloat16),
        "shard",
        scatter_dimension=0,
        tiled=True,
    )
    dense_total, in_total, out_total = (
        butterfly_sum(dense_local, "rep", n_rep, jnp.bfloat16),
        butterfly_sum(gin_local, "rep", n_rep, jnp.bfloat16),
        butterfly_sum(gout_local, "rep", n_rep, jnp.bfloat16),
    )
    return (
        outputs,
        grad_inputs,
        gain1_total,
        dense_total[:, : 3 * width],
        dense_total[:, 3 * width : 4 * width],
        gain2_total,
        dense_total[:, 4 * width :],
        in_total,
        out_total,
    )


def solution(mesh):
    in_specs = (
        P(("shard", "rep"), None),
        P(),
        P("shard", None),
        P("shard", None),
        P(),
        P("shard", None),
        P(None, "shard", None),
        P(None, "shard", None),
        P(("shard", "rep"), None),
        P(),
        P(("shard", "rep"), None),
    )
    out_specs = (
        P(("shard", "rep"), None),
        P(("shard", "rep"), None),
        P(),
        P("shard", None),
        P("shard", None),
        P(),
        P("shard", None),
        P(None, "shard", None),
        P(None, "shard", None),
    )
    return jax.shard_map(body, mesh=mesh, in_specs=in_specs, out_specs=out_specs, check_vma=False)
```

```python
import jax
import jax.numpy as jnp
from jax import lax
from jax.sharding import Mesh, PartitionSpec as P

HEADS = 12
HD = 64
EXPERTS = 32
E_WIN = 2
SEQ = 197
CAP = 128
SHARD = ("chip", "core")


EPS = 1e-06


def layer_norm(values, gain):
    centred = values - jnp.mean(values, axis=-1, keepdims=True)
    inverse = lax.rsqrt(jnp.mean(centred * centred, axis=-1, keepdims=True) + EPS)
    normed = centred * inverse
    return (normed, inverse, (normed * gain).astype(jnp.bfloat16))


def layer_norm_back(grad_out, normed, inverse, gain):
    scaled = grad_out * gain
    grad_in = inverse * (
        scaled
        - jnp.mean(scaled, axis=-1, keepdims=True)
        - normed * jnp.mean(scaled * normed, axis=-1, keepdims=True)
    )
    return (grad_in, jnp.sum(grad_out * normed, axis=0))


def butterfly_sum(value, axis, size, wire=None):
    step = 1
    while step < size:
        pairs = [(i, i ^ step) for i in range(size)]
        sent = value if wire is None else value.astype(wire)
        other = lax.ppermute(sent, axis, pairs)
        value = sent.astype(jnp.float32) + other.astype(jnp.float32)
        step *= 2
    return value


def heads_view(block, images):
    return block.reshape(images, SEQ, HEADS, HD)


def attention_scores(qkv, images):
    width = HEADS * HD
    query = heads_view(qkv[:, :width], images)
    keys = heads_view(qkv[:, width : 2 * width], images)
    values = heads_view(qkv[:, 2 * width :], images)
    scores = jnp.einsum(
        "bqhd,bkhd->bhqk", query, keys, preferred_element_type=jnp.float32
    ) * HD ** (-0.5)
    return (query, keys, values, scores)


def attention_forward(qkv, images):
    query, keys, values, scores = attention_scores(qkv, images)
    logsum = jax.nn.logsumexp(scores, axis=-1, keepdims=True)
    probs = jnp.exp(scores - logsum).astype(jnp.bfloat16)
    mixed = jnp.einsum("bhqk,bkhd->bqhd", probs, values, preferred_element_type=jnp.float32).astype(
        jnp.bfloat16
    )
    return (mixed.reshape(images * SEQ, HEADS * HD), logsum)


def attention_backward(qkv, mixed, logsum, grad_mixed, images):
    query, keys, values, scores = attention_scores(qkv, images)
    probs_full = jnp.exp(scores - logsum)
    probs = probs_full.astype(jnp.bfloat16)
    grad_out = heads_view(grad_mixed, images)
    out_rows = heads_view(mixed, images)
    grad_values = jnp.einsum("bhqk,bqhd->bkhd", probs, grad_out, preferred_element_type=jnp.float32)
    grad_probs = jnp.einsum("bqhd,bkhd->bhqk", grad_out, values, preferred_element_type=jnp.float32)
    delta = jnp.sum(grad_out.astype(jnp.float32) * out_rows.astype(jnp.float32), axis=-1)
    delta = jnp.transpose(delta, (0, 2, 1))[..., None]
    grad_scores = (probs_full * (grad_probs - delta)).astype(jnp.bfloat16)
    scale = HD ** (-0.5)
    grad_query = (
        jnp.einsum("bhqk,bkhd->bqhd", grad_scores, keys, preferred_element_type=jnp.float32) * scale
    )
    grad_keys = (
        jnp.einsum("bhqk,bqhd->bkhd", grad_scores, query, preferred_element_type=jnp.float32)
        * scale
    )
    width = HEADS * HD
    rows = images * SEQ
    return jnp.concatenate(
        [
            grad_query.reshape(rows, width),
            grad_keys.reshape(rows, width),
            grad_values.reshape(rows, width),
        ],
        axis=1,
    ).astype(jnp.bfloat16)


def route_masks(expert_ids, capacity):
    count = expert_ids.shape[0]
    picked_hot = (expert_ids[:, :, None] == jnp.arange(E_WIN)[None, None, :]).astype(jnp.int32)
    ordered = jnp.transpose(picked_hot, (1, 0, 2)).reshape(2 * count, E_WIN)
    before = jnp.cumsum(ordered, axis=0) - ordered
    position = jnp.sum(before * ordered, axis=1).reshape(2, count).T
    limit = jnp.sum(picked_hot * capacity[None, None, :], axis=2)
    kept_mask = (position < limit).astype(jnp.float32)
    slot_hot = (position[:, :, None] == jnp.arange(CAP)[None, None, :]).astype(jnp.float32)
    return (
        kept_mask[:, :, None, None]
        * picked_hot.astype(jnp.float32)[:, :, :, None]
        * slot_hot[:, :, None, :]
    )


def body(
    inputs,
    norm1_gain,
    w_qkv,
    w_proj,
    norm2_gain,
    w_router,
    w_expert_in,
    w_expert_out,
    expert_ids,
    capacity,
    cotangent,
):
    high = lax.Precision.HIGHEST
    images = inputs.shape[0] // SEQ
    shard_rows = w_qkv.shape[0]
    n_chip = lax.axis_size("chip")
    n_core = lax.axis_size("core")
    width = HEADS * HD
    dense_all = lax.all_gather(
        jnp.concatenate([w_qkv, w_proj, w_router], axis=1), SHARD, axis=0, tiled=True
    )
    full_qkv, full_proj, full_router = (
        dense_all[:, : 3 * width],
        dense_all[:, 3 * width : 4 * width],
        dense_all[:, 4 * width :],
    )
    x_float = inputs.astype(jnp.float32)
    normed1, inverse1, hidden1 = layer_norm(x_float, norm1_gain)
    qkv = jnp.dot(hidden1, full_qkv, preferred_element_type=jnp.float32).astype(jnp.bfloat16)
    mixed, logsum = attention_forward(qkv, images)
    attended = x_float + jnp.dot(mixed, full_proj, preferred_element_type=jnp.float32)
    normed2, inverse2, hidden2 = layer_norm(attended, norm2_gain)
    logits = jnp.dot(hidden2, full_router, preferred_element_type=jnp.float32)
    router = jax.nn.softmax(logits, axis=-1)
    expert_hot = (expert_ids[:, :, None] == jnp.arange(EXPERTS)[None, None, :]).astype(jnp.float32)
    gate = jnp.sum(router[:, None, :] * expert_hot, axis=2)
    masks = route_masks(expert_ids, capacity)
    dispatch_float = jnp.sum(masks, axis=1)
    dispatch = dispatch_float.astype(jnp.bfloat16)
    combine = jnp.sum(masks * gate[:, :, None, None], axis=1)
    expert_rows = jnp.einsum(
        "rec,rd->ecd", dispatch, hidden2, preferred_element_type=jnp.float32
    ).astype(jnp.bfloat16)
    w_out_chip = lax.all_gather(w_expert_out, "core", axis=1, tiled=True)
    w_in_part = lax.all_to_all(w_expert_in, "chip", 2, 1, tiled=True)
    w_in_part = w_in_part.reshape(E_WIN, n_chip, shard_rows, -1)
    w_in_chip = lax.all_gather(w_in_part, "core", axis=2, tiled=False).reshape(
        E_WIN, n_chip * n_core * shard_rows, -1
    )
    rows_all = lax.all_gather(expert_rows, "chip", axis=1, tiled=True)
    pre = jnp.einsum("erd,edh->erh", rows_all, w_in_chip, preferred_element_type=jnp.float32)
    activated = jax.nn.gelu(pre, approximate=False).astype(jnp.bfloat16)
    out_part = jnp.einsum(
        "erh,ehd->erd", activated, w_out_chip, preferred_element_type=jnp.float32
    ).astype(jnp.bfloat16)
    expert_out = lax.psum_scatter(out_part, "chip", scatter_dimension=1, tiled=True)
    eout_float = expert_out.astype(jnp.float32)
    moe = jnp.einsum("rec,ecd->rd", combine, eout_float, precision=high)
    outputs = (attended + moe).astype(jnp.bfloat16)
    grad = cotangent.astype(jnp.float32)
    matched = jnp.einsum("rd,ecd->rec", grad, eout_float, precision=high)
    grad_gate = jnp.sum(masks * matched[:, None, :, :], axis=(2, 3))
    grad_eout = jnp.einsum("rec,rd->ecd", combine, grad, precision=high).astype(jnp.bfloat16)
    back_qkv, back_proj, back_router = (full_qkv, full_proj, full_router)
    geout_all = lax.all_gather(grad_eout, "chip", axis=1, tiled=True)
    grad_act = jnp.einsum(
        "erd,ehd->erh", geout_all, w_out_chip, preferred_element_type=jnp.float32
    )
    slope = (
        0.5 * (1.0 + jax.scipy.special.erf(pre * 0.7071067811865476))
        + pre * jnp.exp(-0.5 * pre * pre) * 0.3989422804014327
    )
    grad_pre = (grad_act * slope).astype(jnp.bfloat16)
    rows_part = jnp.einsum(
        "erh,edh->erd", grad_pre, w_in_chip, preferred_element_type=jnp.float32
    ).astype(jnp.bfloat16)
    grad_rows = lax.psum_scatter(rows_part, "chip", scatter_dimension=1, tiled=True)
    gin_chip = jnp.einsum("erd,erh->edh", rows_all, grad_pre, preferred_element_type=jnp.float32)
    gin_chip = gin_chip.astype(jnp.bfloat16).reshape(E_WIN, n_chip, n_core, shard_rows, -1)
    gin_core = lax.psum_scatter(gin_chip, "core", scatter_dimension=2, tiled=True)
    gin_local = lax.all_to_all(gin_core, "chip", 1, 4, tiled=True).reshape(E_WIN, shard_rows, -1)
    gout_chip = jnp.einsum(
        "erh,erd->ehd", activated, geout_all, preferred_element_type=jnp.float32
    ).astype(jnp.bfloat16)
    gout_local = lax.psum_scatter(gout_chip, "core", scatter_dimension=1, tiled=True)
    grad_probs = jnp.sum(grad_gate[:, :, None] * expert_hot, axis=1)
    grad_logits = (
        router * (grad_probs - jnp.sum(router * grad_probs, axis=-1, keepdims=True))
    ).astype(jnp.bfloat16)
    grad_hidden2 = jnp.einsum(
        "rec,ecd->rd", dispatch, grad_rows, preferred_element_type=jnp.float32
    ) + jnp.einsum("re,de->rd", grad_logits, back_router, preferred_element_type=jnp.float32)
    grad_norm2, gain2 = layer_norm_back(grad_hidden2, normed2, inverse2, norm2_gain)
    grad_attended = grad + grad_norm2
    grad_branch = grad_attended.astype(jnp.bfloat16)
    grad_mixed = jnp.einsum(
        "rk,dk->rd", grad_branch, back_proj, preferred_element_type=jnp.float32
    ).astype(jnp.bfloat16)
    grad_qkv_rows = attention_backward(qkv, mixed, logsum, grad_mixed, images)
    grad_hidden1 = jnp.einsum(
        "rk,dk->rd", grad_qkv_rows, back_qkv, preferred_element_type=jnp.float32
    )
    grad_norm1, gain1 = layer_norm_back(grad_hidden1, normed1, inverse1, norm1_gain)
    grad_inputs = grad_attended + grad_norm1
    n_shard = n_chip * n_core
    n_rep = lax.axis_size("rep")
    gains = butterfly_sum(jnp.stack([gain1, gain2]), SHARD, n_shard)
    gains = butterfly_sum(gains, "rep", n_rep)
    gain1_total, gain2_total = gains[0], gains[1]
    dense_local = lax.psum_scatter(
        jnp.concatenate(
            [
                jnp.einsum("rc,rk->ck", hidden1, grad_qkv_rows, preferred_element_type=jnp.float32),
                jnp.einsum("rc,rk->ck", mixed, grad_branch, preferred_element_type=jnp.float32),
                jnp.einsum("rc,rk->ck", hidden2, grad_logits, preferred_element_type=jnp.float32),
            ],
            axis=1,
        ).astype(jnp.bfloat16),
        SHARD,
        scatter_dimension=0,
        tiled=True,
    )
    dense_total, in_total, out_total = (
        butterfly_sum(dense_local, "rep", n_rep, jnp.bfloat16),
        butterfly_sum(gin_local, "rep", n_rep, jnp.bfloat16),
        butterfly_sum(gout_local, "rep", n_rep, jnp.bfloat16),
    )
    return (
        outputs,
        grad_inputs,
        gain1_total,
        dense_total[:, : 3 * width],
        dense_total[:, 3 * width : 4 * width],
        gain2_total,
        dense_total[:, 4 * width :],
        in_total,
        out_total,
    )


def solution(mesh):
    in_specs = (
        P(("chip", "core", "rep"), None),
        P(),
        P(SHARD, None),
        P(SHARD, None),
        P(),
        P(SHARD, None),
        P(None, SHARD, None),
        P(None, SHARD, None),
        P(("chip", "core", "rep"), None),
        P(),
        P(("chip", "core", "rep"), None),
    )
    out_specs = (
        P(("chip", "core", "rep"), None),
        P(("chip", "core", "rep"), None),
        P(),
        P(SHARD, None),
        P(SHARD, None),
        P(),
        P(SHARD, None),
        P(None, SHARD, None),
        P(None, SHARD, None),
    )
    n_shard, n_rep = mesh.devices.shape
    split = Mesh(mesh.devices.reshape(n_shard // 2, 2, n_rep), ("chip", "core", "rep"))
    return jax.shard_map(body, mesh=split, in_specs=in_specs, out_specs=out_specs, check_vma=False)
```

```python
import jax
import jax.numpy as jnp
from jax import lax
from jax.sharding import PartitionSpec as P

HEADS = 12
HD = 64
EXPERTS = 32
E_WIN = 2
SEQ = 197
CAP = 128


EPS = 1e-06


def layer_norm(values, gain):
    centred = values - jnp.mean(values, axis=-1, keepdims=True)
    inverse = lax.rsqrt(jnp.mean(centred * centred, axis=-1, keepdims=True) + EPS)
    normed = centred * inverse
    return (normed, inverse, (normed * gain).astype(jnp.bfloat16))


def layer_norm_back(grad_out, normed, inverse, gain):
    scaled = grad_out * gain
    grad_in = inverse * (
        scaled
        - jnp.mean(scaled, axis=-1, keepdims=True)
        - normed * jnp.mean(scaled * normed, axis=-1, keepdims=True)
    )
    return (grad_in, jnp.sum(grad_out * normed, axis=0))


def butterfly_sum(value, axis, size, wire=None):
    step = 1
    while step < size:
        pairs = [(i, i ^ step) for i in range(size)]
        sent = value if wire is None else value.astype(wire)
        other = lax.ppermute(sent, axis, pairs)
        value = sent.astype(jnp.float32) + other.astype(jnp.float32)
        step *= 2
    return value


def heads_view(block, images):
    return block.reshape(images, SEQ, HEADS, HD)


def attention_scores(qkv, images):
    width = HEADS * HD
    query = heads_view(qkv[:, :width], images)
    keys = heads_view(qkv[:, width : 2 * width], images)
    values = heads_view(qkv[:, 2 * width :], images)
    scores = jnp.einsum(
        "bqhd,bkhd->bhqk", query, keys, preferred_element_type=jnp.float32
    ) * HD ** (-0.5)
    return (query, keys, values, scores)


def attention_forward(qkv, images):
    query, keys, values, scores = attention_scores(qkv, images)
    logsum = jax.nn.logsumexp(scores, axis=-1, keepdims=True)
    probs = jnp.exp(scores - logsum).astype(jnp.bfloat16)
    mixed = jnp.einsum("bhqk,bkhd->bqhd", probs, values, preferred_element_type=jnp.float32).astype(
        jnp.bfloat16
    )
    return (mixed.reshape(images * SEQ, HEADS * HD), logsum)


def attention_backward(qkv, mixed, logsum, grad_mixed, images):
    query, keys, values, scores = attention_scores(qkv, images)
    probs_full = jnp.exp(scores - logsum)
    probs = probs_full.astype(jnp.bfloat16)
    grad_out = heads_view(grad_mixed, images)
    out_rows = heads_view(mixed, images)
    grad_values = jnp.einsum("bhqk,bqhd->bkhd", probs, grad_out, preferred_element_type=jnp.float32)
    grad_probs = jnp.einsum("bqhd,bkhd->bhqk", grad_out, values, preferred_element_type=jnp.float32)
    delta = jnp.sum(grad_out.astype(jnp.float32) * out_rows.astype(jnp.float32), axis=-1)
    delta = jnp.transpose(delta, (0, 2, 1))[..., None]
    grad_scores = (probs_full * (grad_probs - delta)).astype(jnp.bfloat16)
    scale = HD ** (-0.5)
    grad_query = (
        jnp.einsum("bhqk,bkhd->bqhd", grad_scores, keys, preferred_element_type=jnp.float32) * scale
    )
    grad_keys = (
        jnp.einsum("bhqk,bqhd->bkhd", grad_scores, query, preferred_element_type=jnp.float32)
        * scale
    )
    width = HEADS * HD
    rows = images * SEQ
    return jnp.concatenate(
        [
            grad_query.reshape(rows, width),
            grad_keys.reshape(rows, width),
            grad_values.reshape(rows, width),
        ],
        axis=1,
    ).astype(jnp.bfloat16)


def route_masks(expert_ids, capacity):
    count = expert_ids.shape[0]
    picked_hot = (expert_ids[:, :, None] == jnp.arange(E_WIN)[None, None, :]).astype(jnp.int32)
    ordered = jnp.transpose(picked_hot, (1, 0, 2)).reshape(2 * count, E_WIN)
    before = jnp.cumsum(ordered, axis=0) - ordered
    position = jnp.sum(before * ordered, axis=1).reshape(2, count).T
    limit = jnp.sum(picked_hot * capacity[None, None, :], axis=2)
    kept_mask = (position < limit).astype(jnp.float32)
    slot_hot = (position[:, :, None] == jnp.arange(CAP)[None, None, :]).astype(jnp.float32)
    return (
        kept_mask[:, :, None, None]
        * picked_hot.astype(jnp.float32)[:, :, :, None]
        * slot_hot[:, :, None, :]
    )


def body(
    inputs,
    norm1_gain,
    w_qkv,
    w_proj,
    norm2_gain,
    w_router,
    w_expert_in,
    w_expert_out,
    expert_ids,
    capacity,
    cotangent,
):
    high = lax.Precision.HIGHEST
    images = inputs.shape[0] // SEQ
    shard_rows = w_qkv.shape[0]
    hid_rows = w_expert_out.shape[1]
    width = HEADS * HD
    dense_all = lax.all_gather(
        jnp.concatenate([w_qkv, w_proj, w_router], axis=1), "shard", axis=0, tiled=True
    )
    full_qkv, full_proj, full_router = (
        dense_all[:, : 3 * width],
        dense_all[:, 3 * width : 4 * width],
        dense_all[:, 4 * width :],
    )
    x_float = inputs.astype(jnp.float32)
    normed1, inverse1, hidden1 = layer_norm(x_float, norm1_gain)
    qkv = jnp.dot(hidden1, full_qkv, preferred_element_type=jnp.float32).astype(jnp.bfloat16)
    mixed, logsum = attention_forward(qkv, images)
    attended = x_float + jnp.dot(mixed, full_proj, preferred_element_type=jnp.float32)
    normed2, inverse2, hidden2 = layer_norm(attended, norm2_gain)
    logits = jnp.dot(hidden2, full_router, preferred_element_type=jnp.float32)
    router = jax.nn.softmax(logits, axis=-1)
    expert_hot = (expert_ids[:, :, None] == jnp.arange(EXPERTS)[None, None, :]).astype(jnp.float32)
    gate = jnp.sum(router[:, None, :] * expert_hot, axis=2)
    masks = route_masks(expert_ids, capacity)
    dispatch_float = jnp.sum(masks, axis=1)
    dispatch = dispatch_float.astype(jnp.bfloat16)
    combine = jnp.sum(masks * gate[:, :, None, None], axis=1)
    expert_rows = jnp.einsum(
        "rec,rd->ecd", dispatch, hidden2, preferred_element_type=jnp.float32
    ).astype(jnp.bfloat16)
    w_in_cols = lax.all_to_all(w_expert_in, "shard", 2, 1, tiled=True)
    grad = cotangent.astype(jnp.float32)
    grad_eout = jnp.einsum("rec,rd->ecd", combine, grad, precision=high).astype(jnp.bfloat16)
    gathered = lax.all_gather(
        jnp.stack([expert_rows, grad_eout]), "shard", axis=2, tiled=True
    )
    rows_all, geout_all = gathered[0], gathered[1]
    pre = jnp.einsum("erd,edh->erh", rows_all, w_in_cols, preferred_element_type=jnp.float32)
    activated = jax.nn.gelu(pre, approximate=False).astype(jnp.bfloat16)
    out_part = jnp.einsum(
        "erh,ehd->erd", activated, w_expert_out, preferred_element_type=jnp.float32
    ).astype(jnp.bfloat16)
    grad_act = jnp.einsum(
        "erd,ehd->erh", geout_all, w_expert_out, preferred_element_type=jnp.float32
    )
    slope = (
        0.5 * (1.0 + jax.scipy.special.erf(pre * 0.7071067811865476))
        + pre * jnp.exp(-0.5 * pre * pre) * 0.3989422804014327
    )
    grad_pre = (grad_act * slope).astype(jnp.bfloat16)
    rows_part = jnp.einsum(
        "erh,edh->erd", grad_pre, w_in_cols, preferred_element_type=jnp.float32
    ).astype(jnp.bfloat16)
    scattered = lax.psum_scatter(
        jnp.stack([out_part, rows_part]), "shard", scatter_dimension=2, tiled=True
    )
    expert_out, grad_rows = scattered[0], scattered[1]
    eout_float = expert_out.astype(jnp.float32)
    moe = jnp.einsum("rec,ecd->rd", combine, eout_float, precision=high)
    outputs = (attended + moe).astype(jnp.bfloat16)
    matched = jnp.einsum("rd,ecd->rec", grad, eout_float, precision=high)
    grad_gate = jnp.sum(masks * matched[:, None, :, :], axis=(2, 3))
    back_qkv, back_proj, back_router = (full_qkv, full_proj, full_router)
    gin_cols = jnp.einsum("erd,erh->edh", rows_all, grad_pre, preferred_element_type=jnp.float32)
    gin_local = lax.all_to_all(gin_cols.astype(jnp.bfloat16), "shard", 1, 2, tiled=True)
    gout_local = jnp.einsum(
        "erh,erd->ehd", activated, geout_all, preferred_element_type=jnp.float32
    ).astype(jnp.bfloat16)
    grad_probs = jnp.sum(grad_gate[:, :, None] * expert_hot, axis=1)
    grad_logits = (
        router * (grad_probs - jnp.sum(router * grad_probs, axis=-1, keepdims=True))
    ).astype(jnp.bfloat16)
    grad_hidden2 = jnp.einsum(
        "rec,ecd->rd", dispatch, grad_rows, preferred_element_type=jnp.float32
    ) + jnp.einsum("re,de->rd", grad_logits, back_router, preferred_element_type=jnp.float32)
    grad_norm2, gain2 = layer_norm_back(grad_hidden2, normed2, inverse2, norm2_gain)
    grad_attended = grad + grad_norm2
    grad_branch = grad_attended.astype(jnp.bfloat16)
    grad_mixed = jnp.einsum(
        "rk,dk->rd", grad_branch, back_proj, preferred_element_type=jnp.float32
    ).astype(jnp.bfloat16)
    grad_qkv_rows = attention_backward(qkv, mixed, logsum, grad_mixed, images)
    grad_hidden1 = jnp.einsum(
        "rk,dk->rd", grad_qkv_rows, back_qkv, preferred_element_type=jnp.float32
    )
    grad_norm1, gain1 = layer_norm_back(grad_hidden1, normed1, inverse1, norm1_gain)
    grad_inputs = grad_attended + grad_norm1
    n_shard = lax.axis_size("shard")
    n_rep = lax.axis_size("rep")
    gains = butterfly_sum(jnp.stack([gain1, gain2]), "shard", n_shard)
    gains = butterfly_sum(gains, "rep", n_rep)
    gain1_total, gain2_total = gains[0], gains[1]
    dense_local = lax.psum_scatter(
        jnp.concatenate(
            [
                jnp.einsum("rc,rk->ck", hidden1, grad_qkv_rows, preferred_element_type=jnp.float32),
                jnp.einsum("rc,rk->ck", mixed, grad_branch, preferred_element_type=jnp.float32),
                jnp.einsum("rc,rk->ck", hidden2, grad_logits, preferred_element_type=jnp.float32),
            ],
            axis=1,
        ).astype(jnp.bfloat16),
        "shard",
        scatter_dimension=0,
        tiled=True,
    )
    dense_total, in_total, out_total = (
        butterfly_sum(dense_local, "rep", n_rep, jnp.bfloat16),
        butterfly_sum(gin_local, "rep", n_rep, jnp.bfloat16),
        butterfly_sum(gout_local, "rep", n_rep, jnp.bfloat16),
    )
    return (
        outputs,
        grad_inputs,
        gain1_total,
        dense_total[:, : 3 * width],
        dense_total[:, 3 * width : 4 * width],
        gain2_total,
        dense_total[:, 4 * width :],
        in_total,
        out_total,
    )


def solution(mesh):
    in_specs = (
        P(("shard", "rep"), None),
        P(),
        P("shard", None),
        P("shard", None),
        P(),
        P("shard", None),
        P(None, "shard", None),
        P(None, "shard", None),
        P(("shard", "rep"), None),
        P(),
        P(("shard", "rep"), None),
    )
    out_specs = (
        P(("shard", "rep"), None),
        P(("shard", "rep"), None),
        P(),
        P("shard", None),
        P("shard", None),
        P(),
        P("shard", None),
        P(None, "shard", None),
        P(None, "shard", None),
    )
    return jax.shard_map(body, mesh=mesh, in_specs=in_specs, out_specs=out_specs, check_vma=False)
```

```python
import jax
import jax.numpy as jnp
from jax import lax
from jax.experimental import pallas as pl
from jax.sharding import PartitionSpec as P

HEADS = 12
HD = 64
EXPERTS = 32
E_WIN = 2
SEQ = 197
CAP = 128


EPS = 1e-06
ROW_TILE = 256

def expert_kernel(rows_ref, geout_ref, w_in_ref, w_out_ref, parts_ref, act_ref, gpre_ref):
    rows = rows_ref[...]
    w_in = w_in_ref[...]
    w_out = w_out_ref[...]
    pre = jnp.dot(rows, w_in, preferred_element_type=jnp.float32)
    erf_term = lax.erf(pre * 0.7071067811865476)
    activated = (0.5 * pre * (1.0 + erf_term)).astype(jnp.bfloat16)
    act_ref[...] = activated
    parts_ref[0] = jnp.dot(activated, w_out, preferred_element_type=jnp.float32).astype(jnp.bfloat16)
    grad_act = lax.dot_general(
        geout_ref[...], w_out, (((1,), (1,)), ((), ())), preferred_element_type=jnp.float32
    )
    slope = 0.5 * (1.0 + erf_term) + pre * jnp.exp(-0.5 * pre * pre) * 0.3989422804014327
    grad_pre = (grad_act * slope).astype(jnp.bfloat16)
    gpre_ref[...] = grad_pre
    parts_ref[1] = lax.dot_general(
        grad_pre, w_in, (((1,), (1,)), ((), ())), preferred_element_type=jnp.float32
    ).astype(jnp.bfloat16)

def expert_block(gathered, w_in_cols, w_out):
    _, experts, rows, width = gathered.shape
    hidden = w_in_cols.shape[2]
    grid = (experts, rows // ROW_TILE)
    return pl.pallas_call(
        expert_kernel,
        grid=grid,
        in_specs=[
            pl.BlockSpec((None, None, ROW_TILE, width), lambda e, i: (0, e, i, 0)),
            pl.BlockSpec((None, None, ROW_TILE, width), lambda e, i: (1, e, i, 0)),
            pl.BlockSpec((None, width, hidden), lambda e, i: (e, 0, 0)),
            pl.BlockSpec((None, hidden, width), lambda e, i: (e, 0, 0)),
        ],
        out_specs=[
            pl.BlockSpec((2, None, ROW_TILE, width), lambda e, i: (0, e, i, 0)),
            pl.BlockSpec((None, ROW_TILE, hidden), lambda e, i: (e, i, 0)),
            pl.BlockSpec((None, ROW_TILE, hidden), lambda e, i: (e, i, 0)),
        ],
        out_shape=[
            jax.ShapeDtypeStruct((2, experts, rows, width), jnp.bfloat16),
            jax.ShapeDtypeStruct((experts, rows, hidden), jnp.bfloat16),
            jax.ShapeDtypeStruct((experts, rows, hidden), jnp.bfloat16),
        ],
    )(gathered, gathered, w_in_cols, w_out)


def layer_norm(values, gain):
    centred = values - jnp.mean(values, axis=-1, keepdims=True)
    inverse = lax.rsqrt(jnp.mean(centred * centred, axis=-1, keepdims=True) + EPS)
    normed = centred * inverse
    return (normed, inverse, (normed * gain).astype(jnp.bfloat16))


def layer_norm_back(grad_out, normed, inverse, gain):
    scaled = grad_out * gain
    grad_in = inverse * (
        scaled
        - jnp.mean(scaled, axis=-1, keepdims=True)
        - normed * jnp.mean(scaled * normed, axis=-1, keepdims=True)
    )
    return (grad_in, jnp.sum(grad_out * normed, axis=0))


def butterfly_sum(value, axis, size, wire=None):
    step = 1
    while step < size:
        pairs = [(i, i ^ step) for i in range(size)]
        sent = value if wire is None else value.astype(wire)
        other = lax.ppermute(sent, axis, pairs)
        value = sent.astype(jnp.float32) + other.astype(jnp.float32)
        step *= 2
    return value


def heads_view(block, images):
    return block.reshape(images, SEQ, HEADS, HD)


def attention_scores(qkv, images):
    width = HEADS * HD
    query = heads_view(qkv[:, :width], images)
    keys = heads_view(qkv[:, width : 2 * width], images)
    values = heads_view(qkv[:, 2 * width :], images)
    scores = jnp.einsum(
        "bqhd,bkhd->bhqk", query, keys, preferred_element_type=jnp.float32
    ) * HD ** (-0.5)
    return (query, keys, values, scores)


def attention_forward(qkv, images):
    query, keys, values, scores = attention_scores(qkv, images)
    logsum = jax.nn.logsumexp(scores, axis=-1, keepdims=True)
    probs = jnp.exp(scores - logsum).astype(jnp.bfloat16)
    mixed = jnp.einsum("bhqk,bkhd->bqhd", probs, values, preferred_element_type=jnp.float32).astype(
        jnp.bfloat16
    )
    return (mixed.reshape(images * SEQ, HEADS * HD), logsum)


def attention_backward(qkv, mixed, logsum, grad_mixed, images):
    query, keys, values, scores = attention_scores(qkv, images)
    probs_full = jnp.exp(scores - logsum)
    probs = probs_full.astype(jnp.bfloat16)
    grad_out = heads_view(grad_mixed, images)
    out_rows = heads_view(mixed, images)
    grad_values = jnp.einsum("bhqk,bqhd->bkhd", probs, grad_out, preferred_element_type=jnp.float32)
    grad_probs = jnp.einsum("bqhd,bkhd->bhqk", grad_out, values, preferred_element_type=jnp.float32)
    delta = jnp.sum(grad_out.astype(jnp.float32) * out_rows.astype(jnp.float32), axis=-1)
    delta = jnp.transpose(delta, (0, 2, 1))[..., None]
    grad_scores = (probs_full * (grad_probs - delta)).astype(jnp.bfloat16)
    scale = HD ** (-0.5)
    grad_query = (
        jnp.einsum("bhqk,bkhd->bqhd", grad_scores, keys, preferred_element_type=jnp.float32) * scale
    )
    grad_keys = (
        jnp.einsum("bhqk,bqhd->bkhd", grad_scores, query, preferred_element_type=jnp.float32)
        * scale
    )
    width = HEADS * HD
    rows = images * SEQ
    return jnp.concatenate(
        [
            grad_query.reshape(rows, width),
            grad_keys.reshape(rows, width),
            grad_values.reshape(rows, width),
        ],
        axis=1,
    ).astype(jnp.bfloat16)


def route_masks(expert_ids, capacity):
    count = expert_ids.shape[0]
    picked_hot = (expert_ids[:, :, None] == jnp.arange(E_WIN)[None, None, :]).astype(jnp.int32)
    ordered = jnp.transpose(picked_hot, (1, 0, 2)).reshape(2 * count, E_WIN)
    before = jnp.cumsum(ordered, axis=0) - ordered
    position = jnp.sum(before * ordered, axis=1).reshape(2, count).T
    limit = jnp.sum(picked_hot * capacity[None, None, :], axis=2)
    kept_mask = (position < limit).astype(jnp.float32)
    slot_hot = (position[:, :, None] == jnp.arange(CAP)[None, None, :]).astype(jnp.float32)
    return (
        kept_mask[:, :, None, None]
        * picked_hot.astype(jnp.float32)[:, :, :, None]
        * slot_hot[:, :, None, :]
    )


def body(
    inputs,
    norm1_gain,
    w_qkv,
    w_proj,
    norm2_gain,
    w_router,
    w_expert_in,
    w_expert_out,
    expert_ids,
    capacity,
    cotangent,
):
    high = lax.Precision.HIGHEST
    images = inputs.shape[0] // SEQ
    shard_rows = w_qkv.shape[0]
    hid_rows = w_expert_out.shape[1]
    width = HEADS * HD
    dense_all = lax.all_gather(
        jnp.concatenate([w_qkv, w_proj, w_router], axis=1), "shard", axis=0, tiled=True
    )
    full_qkv, full_proj, full_router = (
        dense_all[:, : 3 * width],
        dense_all[:, 3 * width : 4 * width],
        dense_all[:, 4 * width :],
    )
    x_float = inputs.astype(jnp.float32)
    normed1, inverse1, hidden1 = layer_norm(x_float, norm1_gain)
    qkv = jnp.dot(hidden1, full_qkv, preferred_element_type=jnp.float32).astype(jnp.bfloat16)
    mixed, logsum = attention_forward(qkv, images)
    attended = x_float + jnp.dot(mixed, full_proj, preferred_element_type=jnp.float32)
    normed2, inverse2, hidden2 = layer_norm(attended, norm2_gain)
    logits = jnp.dot(hidden2, full_router, preferred_element_type=jnp.float32)
    router = jax.nn.softmax(logits, axis=-1)
    expert_hot = (expert_ids[:, :, None] == jnp.arange(EXPERTS)[None, None, :]).astype(jnp.float32)
    gate = jnp.sum(router[:, None, :] * expert_hot, axis=2)
    masks = route_masks(expert_ids, capacity)
    dispatch_float = jnp.sum(masks, axis=1)
    dispatch = dispatch_float.astype(jnp.bfloat16)
    combine = jnp.sum(masks * gate[:, :, None, None], axis=1)
    expert_rows = jnp.einsum(
        "rec,rd->ecd", dispatch, hidden2, preferred_element_type=jnp.float32
    ).astype(jnp.bfloat16)
    w_in_cols = lax.all_to_all(w_expert_in, "shard", 2, 1, tiled=True)
    grad = cotangent.astype(jnp.float32)
    grad_eout = jnp.einsum("rec,rd->ecd", combine, grad, precision=high).astype(jnp.bfloat16)
    gathered = lax.all_gather(
        jnp.stack([expert_rows, grad_eout]), "shard", axis=2, tiled=True
    )
    rows_all, geout_all = gathered[0], gathered[1]
    parts, activated, grad_pre = expert_block(gathered, w_in_cols, w_expert_out)
    scattered = lax.psum_scatter(parts, "shard", scatter_dimension=2, tiled=True)
    expert_out, grad_rows = scattered[0], scattered[1]
    eout_float = expert_out.astype(jnp.float32)
    moe = jnp.einsum("rec,ecd->rd", combine, eout_float, precision=high)
    outputs = (attended + moe).astype(jnp.bfloat16)
    matched = jnp.einsum("rd,ecd->rec", grad, eout_float, precision=high)
    grad_gate = jnp.sum(masks * matched[:, None, :, :], axis=(2, 3))
    back_qkv, back_proj, back_router = (full_qkv, full_proj, full_router)
    gin_cols = jnp.einsum("erd,erh->edh", rows_all, grad_pre, preferred_element_type=jnp.float32)
    gin_local = lax.all_to_all(gin_cols.astype(jnp.bfloat16), "shard", 1, 2, tiled=True)
    gout_local = jnp.einsum(
        "erh,erd->ehd", activated, geout_all, preferred_element_type=jnp.float32
    ).astype(jnp.bfloat16)
    grad_probs = jnp.sum(grad_gate[:, :, None] * expert_hot, axis=1)
    grad_logits = (
        router * (grad_probs - jnp.sum(router * grad_probs, axis=-1, keepdims=True))
    ).astype(jnp.bfloat16)
    grad_hidden2 = jnp.einsum(
        "rec,ecd->rd", dispatch, grad_rows, preferred_element_type=jnp.float32
    ) + jnp.einsum("re,de->rd", grad_logits, back_router, preferred_element_type=jnp.float32)
    grad_norm2, gain2 = layer_norm_back(grad_hidden2, normed2, inverse2, norm2_gain)
    grad_attended = grad + grad_norm2
    grad_branch = grad_attended.astype(jnp.bfloat16)
    grad_mixed = jnp.einsum(
        "rk,dk->rd", grad_branch, back_proj, preferred_element_type=jnp.float32
    ).astype(jnp.bfloat16)
    grad_qkv_rows = attention_backward(qkv, mixed, logsum, grad_mixed, images)
    grad_hidden1 = jnp.einsum(
        "rk,dk->rd", grad_qkv_rows, back_qkv, preferred_element_type=jnp.float32
    )
    grad_norm1, gain1 = layer_norm_back(grad_hidden1, normed1, inverse1, norm1_gain)
    grad_inputs = grad_attended + grad_norm1
    n_shard = lax.axis_size("shard")
    n_rep = lax.axis_size("rep")
    gains = butterfly_sum(jnp.stack([gain1, gain2]), "shard", n_shard)
    gains = butterfly_sum(gains, "rep", n_rep)
    gain1_total, gain2_total = gains[0], gains[1]
    dense_local = lax.psum_scatter(
        jnp.concatenate(
            [
                jnp.einsum("rc,rk->ck", hidden1, grad_qkv_rows, preferred_element_type=jnp.float32),
                jnp.einsum("rc,rk->ck", mixed, grad_branch, preferred_element_type=jnp.float32),
                jnp.einsum("rc,rk->ck", hidden2, grad_logits, preferred_element_type=jnp.float32),
            ],
            axis=1,
        ).astype(jnp.bfloat16),
        "shard",
        scatter_dimension=0,
        tiled=True,
    )
    dense_total, in_total, out_total = (
        butterfly_sum(dense_local, "rep", n_rep, jnp.bfloat16),
        butterfly_sum(gin_local, "rep", n_rep, jnp.bfloat16),
        butterfly_sum(gout_local, "rep", n_rep, jnp.bfloat16),
    )
    return (
        outputs,
        grad_inputs,
        gain1_total,
        dense_total[:, : 3 * width],
        dense_total[:, 3 * width : 4 * width],
        gain2_total,
        dense_total[:, 4 * width :],
        in_total,
        out_total,
    )


def solution(mesh):
    in_specs = (
        P(("shard", "rep"), None),
        P(),
        P("shard", None),
        P("shard", None),
        P(),
        P("shard", None),
        P(None, "shard", None),
        P(None, "shard", None),
        P(("shard", "rep"), None),
        P(),
        P(("shard", "rep"), None),
    )
    out_specs = (
        P(("shard", "rep"), None),
        P(("shard", "rep"), None),
        P(),
        P("shard", None),
        P("shard", None),
        P(),
        P("shard", None),
        P(None, "shard", None),
        P(None, "shard", None),
    )
    return jax.shard_map(body, mesh=mesh, in_specs=in_specs, out_specs=out_specs, check_vma=False)
```

```python
import jax
import jax.numpy as jnp
from jax import lax
from jax.experimental import pallas as pl
from jax.sharding import PartitionSpec as P

HEADS = 12
HD = 64
EXPERTS = 32
E_WIN = 2
SEQ = 197
CAP = 128


EPS = 1e-06
ROW_TILE = 512

def expert_kernel(rows_ref, geout_ref, w_in_ref, w_out_ref, parts_ref, act_ref, gpre_ref):
    rows = rows_ref[...]
    w_in = w_in_ref[...]
    w_out = w_out_ref[...]
    pre = jnp.dot(rows, w_in, preferred_element_type=jnp.float32)
    erf_term = lax.erf(pre * 0.7071067811865476)
    activated = (0.5 * pre * (1.0 + erf_term)).astype(jnp.bfloat16)
    act_ref[...] = activated
    parts_ref[0] = jnp.dot(activated, w_out, preferred_element_type=jnp.float32).astype(jnp.bfloat16)
    grad_act = lax.dot_general(
        geout_ref[...], w_out, (((1,), (1,)), ((), ())), preferred_element_type=jnp.float32
    )
    slope = 0.5 * (1.0 + erf_term) + pre * jnp.exp(-0.5 * pre * pre) * 0.3989422804014327
    grad_pre = (grad_act * slope).astype(jnp.bfloat16)
    gpre_ref[...] = grad_pre
    parts_ref[1] = lax.dot_general(
        grad_pre, w_in, (((1,), (1,)), ((), ())), preferred_element_type=jnp.float32
    ).astype(jnp.bfloat16)

def expert_block(gathered, w_in_cols, w_out):
    _, experts, rows, width = gathered.shape
    hidden = w_in_cols.shape[2]
    grid = (experts, rows // ROW_TILE)
    return pl.pallas_call(
        expert_kernel,
        grid=grid,
        in_specs=[
            pl.BlockSpec((None, None, ROW_TILE, width), lambda e, i: (0, e, i, 0)),
            pl.BlockSpec((None, None, ROW_TILE, width), lambda e, i: (1, e, i, 0)),
            pl.BlockSpec((None, width, hidden), lambda e, i: (e, 0, 0)),
            pl.BlockSpec((None, hidden, width), lambda e, i: (e, 0, 0)),
        ],
        out_specs=[
            pl.BlockSpec((2, None, ROW_TILE, width), lambda e, i: (0, e, i, 0)),
            pl.BlockSpec((None, ROW_TILE, hidden), lambda e, i: (e, i, 0)),
            pl.BlockSpec((None, ROW_TILE, hidden), lambda e, i: (e, i, 0)),
        ],
        out_shape=[
            jax.ShapeDtypeStruct((2, experts, rows, width), jnp.bfloat16),
            jax.ShapeDtypeStruct((experts, rows, hidden), jnp.bfloat16),
            jax.ShapeDtypeStruct((experts, rows, hidden), jnp.bfloat16),
        ],
    )(gathered, gathered, w_in_cols, w_out)


def layer_norm(values, gain):
    centred = values - jnp.mean(values, axis=-1, keepdims=True)
    inverse = lax.rsqrt(jnp.mean(centred * centred, axis=-1, keepdims=True) + EPS)
    normed = centred * inverse
    return (normed, inverse, (normed * gain).astype(jnp.bfloat16))


def layer_norm_back(grad_out, normed, inverse, gain):
    scaled = grad_out * gain
    grad_in = inverse * (
        scaled
        - jnp.mean(scaled, axis=-1, keepdims=True)
        - normed * jnp.mean(scaled * normed, axis=-1, keepdims=True)
    )
    return (grad_in, jnp.sum(grad_out * normed, axis=0))


def butterfly_sum(value, axis, size, wire=None):
    step = 1
    while step < size:
        radix = 4 if (size // step) % 4 == 0 else 2
        sent = value if wire is None else value.astype(wire)
        got = [
            lax.ppermute(sent, axis, [(i, i ^ (shift * step)) for i in range(size)]).astype(jnp.float32)
            for shift in range(1, radix)
        ]
        value = sent.astype(jnp.float32) + got[0]
        if radix == 4:
            value = value + (got[1] + got[2])
        step *= radix
    return value


def heads_view(block, images):
    return block.reshape(images, SEQ, HEADS, HD)


def attention_scores(qkv, images):
    width = HEADS * HD
    query = heads_view(qkv[:, :width], images)
    keys = heads_view(qkv[:, width : 2 * width], images)
    values = heads_view(qkv[:, 2 * width :], images)
    scores = jnp.einsum(
        "bqhd,bkhd->bhqk", query, keys, preferred_element_type=jnp.float32
    ) * HD ** (-0.5)
    return (query, keys, values, scores)


def attention_forward(qkv, images):
    query, keys, values, scores = attention_scores(qkv, images)
    logsum = jax.nn.logsumexp(scores, axis=-1, keepdims=True)
    probs = jnp.exp(scores - logsum).astype(jnp.bfloat16)
    mixed = jnp.einsum("bhqk,bkhd->bqhd", probs, values, preferred_element_type=jnp.float32).astype(
        jnp.bfloat16
    )
    return (mixed.reshape(images * SEQ, HEADS * HD), logsum)


def attention_backward(qkv, mixed, logsum, grad_mixed, images):
    query, keys, values, scores = attention_scores(qkv, images)
    probs_full = jnp.exp(scores - logsum)
    probs = probs_full.astype(jnp.bfloat16)
    grad_out = heads_view(grad_mixed, images)
    out_rows = heads_view(mixed, images)
    grad_values = jnp.einsum("bhqk,bqhd->bkhd", probs, grad_out, preferred_element_type=jnp.float32)
    grad_probs = jnp.einsum("bqhd,bkhd->bhqk", grad_out, values, preferred_element_type=jnp.float32)
    delta = jnp.sum(grad_out.astype(jnp.float32) * out_rows.astype(jnp.float32), axis=-1)
    delta = jnp.transpose(delta, (0, 2, 1))[..., None]
    grad_scores = (probs_full * (grad_probs - delta)).astype(jnp.bfloat16)
    scale = HD ** (-0.5)
    grad_query = (
        jnp.einsum("bhqk,bkhd->bqhd", grad_scores, keys, preferred_element_type=jnp.float32) * scale
    )
    grad_keys = (
        jnp.einsum("bhqk,bqhd->bkhd", grad_scores, query, preferred_element_type=jnp.float32)
        * scale
    )
    width = HEADS * HD
    rows = images * SEQ
    return jnp.concatenate(
        [
            grad_query.reshape(rows, width),
            grad_keys.reshape(rows, width),
            grad_values.reshape(rows, width),
        ],
        axis=1,
    ).astype(jnp.bfloat16)


def route_masks(expert_ids, capacity):
    count = expert_ids.shape[0]
    picked_hot = (expert_ids[:, :, None] == jnp.arange(E_WIN)[None, None, :]).astype(jnp.int32)
    ordered = jnp.transpose(picked_hot, (1, 0, 2)).reshape(2 * count, E_WIN)
    before = jnp.cumsum(ordered, axis=0) - ordered
    position = jnp.sum(before * ordered, axis=1).reshape(2, count).T
    limit = jnp.sum(picked_hot * capacity[None, None, :], axis=2)
    kept_mask = (position < limit).astype(jnp.float32)
    slot_hot = (position[:, :, None] == jnp.arange(CAP)[None, None, :]).astype(jnp.float32)
    return (
        kept_mask[:, :, None, None]
        * picked_hot.astype(jnp.float32)[:, :, :, None]
        * slot_hot[:, :, None, :]
    )


def body(
    inputs,
    norm1_gain,
    w_qkv,
    w_proj,
    norm2_gain,
    w_router,
    w_expert_in,
    w_expert_out,
    expert_ids,
    capacity,
    cotangent,
):
    high = lax.Precision.HIGHEST
    images = inputs.shape[0] // SEQ
    shard_rows = w_qkv.shape[0]
    hid_rows = w_expert_out.shape[1]
    width = HEADS * HD
    dense_all = lax.all_gather(
        jnp.concatenate([w_qkv, w_proj, w_router], axis=1), "shard", axis=0, tiled=True
    )
    full_qkv, full_proj, full_router = (
        dense_all[:, : 3 * width],
        dense_all[:, 3 * width : 4 * width],
        dense_all[:, 4 * width :],
    )
    x_float = inputs.astype(jnp.float32)
    normed1, inverse1, hidden1 = layer_norm(x_float, norm1_gain)
    qkv = jnp.dot(hidden1, full_qkv, preferred_element_type=jnp.float32).astype(jnp.bfloat16)
    mixed, logsum = attention_forward(qkv, images)
    attended = x_float + jnp.dot(mixed, full_proj, preferred_element_type=jnp.float32)
    normed2, inverse2, hidden2 = layer_norm(attended, norm2_gain)
    logits = jnp.dot(hidden2, full_router, preferred_element_type=jnp.float32)
    router = jax.nn.softmax(logits, axis=-1)
    expert_hot = (expert_ids[:, :, None] == jnp.arange(EXPERTS)[None, None, :]).astype(jnp.float32)
    gate = jnp.sum(router[:, None, :] * expert_hot, axis=2)
    masks = route_masks(expert_ids, capacity)
    dispatch_float = jnp.sum(masks, axis=1)
    dispatch = dispatch_float.astype(jnp.bfloat16)
    combine = jnp.sum(masks * gate[:, :, None, None], axis=1)
    expert_rows = jnp.einsum(
        "rec,rd->ecd", dispatch, hidden2, preferred_element_type=jnp.float32
    ).astype(jnp.bfloat16)
    w_in_cols = lax.all_to_all(w_expert_in, "shard", 2, 1, tiled=True)
    grad = cotangent.astype(jnp.float32)
    grad_eout = jnp.einsum("rec,rd->ecd", combine, grad, precision=high).astype(jnp.bfloat16)
    gathered = lax.all_gather(
        jnp.stack([expert_rows, grad_eout]), "shard", axis=2, tiled=True
    )
    rows_all, geout_all = gathered[0], gathered[1]
    parts, activated, grad_pre = expert_block(gathered, w_in_cols, w_expert_out)
    scattered = lax.psum_scatter(parts, "shard", scatter_dimension=2, tiled=True)
    expert_out, grad_rows = scattered[0], scattered[1]
    eout_float = expert_out.astype(jnp.float32)
    moe = jnp.einsum("rec,ecd->rd", combine, eout_float, precision=high)
    outputs = (attended + moe).astype(jnp.bfloat16)
    matched = jnp.einsum("rd,ecd->rec", grad, eout_float, precision=high)
    grad_gate = jnp.sum(masks * matched[:, None, :, :], axis=(2, 3))
    back_qkv, back_proj, back_router = (full_qkv, full_proj, full_router)
    gin_cols = jnp.einsum("erd,erh->edh", rows_all, grad_pre, preferred_element_type=jnp.float32)
    gin_local = lax.all_to_all(gin_cols.astype(jnp.bfloat16), "shard", 1, 2, tiled=True)
    gout_local = jnp.einsum(
        "erh,erd->ehd", activated, geout_all, preferred_element_type=jnp.float32
    ).astype(jnp.bfloat16)
    grad_probs = jnp.sum(grad_gate[:, :, None] * expert_hot, axis=1)
    grad_logits = (
        router * (grad_probs - jnp.sum(router * grad_probs, axis=-1, keepdims=True))
    ).astype(jnp.bfloat16)
    grad_hidden2 = jnp.einsum(
        "rec,ecd->rd", dispatch, grad_rows, preferred_element_type=jnp.float32
    ) + jnp.einsum("re,de->rd", grad_logits, back_router, preferred_element_type=jnp.float32)
    grad_norm2, gain2 = layer_norm_back(grad_hidden2, normed2, inverse2, norm2_gain)
    grad_attended = grad + grad_norm2
    grad_branch = grad_attended.astype(jnp.bfloat16)
    grad_mixed = jnp.einsum(
        "rk,dk->rd", grad_branch, back_proj, preferred_element_type=jnp.float32
    ).astype(jnp.bfloat16)
    grad_qkv_rows = attention_backward(qkv, mixed, logsum, grad_mixed, images)
    grad_hidden1 = jnp.einsum(
        "rk,dk->rd", grad_qkv_rows, back_qkv, preferred_element_type=jnp.float32
    )
    grad_norm1, gain1 = layer_norm_back(grad_hidden1, normed1, inverse1, norm1_gain)
    grad_inputs = grad_attended + grad_norm1
    n_shard = lax.axis_size("shard")
    n_rep = lax.axis_size("rep")
    gains = butterfly_sum(jnp.stack([gain1, gain2]), "shard", n_shard)
    gains = butterfly_sum(gains, "rep", n_rep)
    gain1_total, gain2_total = gains[0], gains[1]
    dense_local = lax.psum_scatter(
        jnp.concatenate(
            [
                jnp.einsum("rc,rk->ck", hidden1, grad_qkv_rows, preferred_element_type=jnp.float32),
                jnp.einsum("rc,rk->ck", mixed, grad_branch, preferred_element_type=jnp.float32),
                jnp.einsum("rc,rk->ck", hidden2, grad_logits, preferred_element_type=jnp.float32),
            ],
            axis=1,
        ).astype(jnp.bfloat16),
        "shard",
        scatter_dimension=0,
        tiled=True,
    )
    dense_total, in_total, out_total = (
        butterfly_sum(dense_local, "rep", n_rep, jnp.bfloat16),
        butterfly_sum(gin_local, "rep", n_rep, jnp.bfloat16),
        butterfly_sum(gout_local, "rep", n_rep, jnp.bfloat16),
    )
    return (
        outputs,
        grad_inputs,
        gain1_total,
        dense_total[:, : 3 * width],
        dense_total[:, 3 * width : 4 * width],
        gain2_total,
        dense_total[:, 4 * width :],
        in_total,
        out_total,
    )


def solution(mesh):
    in_specs = (
        P(("shard", "rep"), None),
        P(),
        P("shard", None),
        P("shard", None),
        P(),
        P("shard", None),
        P(None, "shard", None),
        P(None, "shard", None),
        P(("shard", "rep"), None),
        P(),
        P(("shard", "rep"), None),
    )
    out_specs = (
        P(("shard", "rep"), None),
        P(("shard", "rep"), None),
        P(),
        P("shard", None),
        P("shard", None),
        P(),
        P("shard", None),
        P(None, "shard", None),
        P(None, "shard", None),
    )
    return jax.shard_map(body, mesh=mesh, in_specs=in_specs, out_specs=out_specs, check_vma=False)
```

```python
import jax
import jax.numpy as jnp
from jax import lax
from jax.experimental import pallas as pl
from jax.sharding import PartitionSpec as P

HEADS = 12
HD = 64
EXPERTS = 32
E_WIN = 2
SEQ = 197
CAP = 128


EPS = 1e-06
ROW_TILE = 512

def expert_kernel(rows_ref, geout_ref, w_in_ref, w_out_ref, parts_ref, act_ref, gpre_ref):
    rows = rows_ref[...]
    w_in = w_in_ref[...]
    w_out = w_out_ref[...]
    pre = jnp.dot(rows, w_in, preferred_element_type=jnp.float32)
    erf_term = lax.erf(pre * 0.7071067811865476)
    activated = (0.5 * pre * (1.0 + erf_term)).astype(jnp.bfloat16)
    act_ref[...] = activated
    parts_ref[0] = jnp.dot(activated, w_out, preferred_element_type=jnp.float32).astype(jnp.bfloat16)
    grad_act = lax.dot_general(
        geout_ref[...], w_out, (((1,), (1,)), ((), ())), preferred_element_type=jnp.float32
    )
    slope = 0.5 * (1.0 + erf_term) + pre * jnp.exp(-0.5 * pre * pre) * 0.3989422804014327
    grad_pre = (grad_act * slope).astype(jnp.bfloat16)
    gpre_ref[...] = grad_pre
    parts_ref[1] = lax.dot_general(
        grad_pre, w_in, (((1,), (1,)), ((), ())), preferred_element_type=jnp.float32
    ).astype(jnp.bfloat16)

def expert_block(gathered, w_in_cols, w_out):
    _, experts, rows, width = gathered.shape
    hidden = w_in_cols.shape[2]
    grid = (experts, rows // ROW_TILE)
    return pl.pallas_call(
        expert_kernel,
        grid=grid,
        in_specs=[
            pl.BlockSpec((None, None, ROW_TILE, width), lambda e, i: (0, e, i, 0)),
            pl.BlockSpec((None, None, ROW_TILE, width), lambda e, i: (1, e, i, 0)),
            pl.BlockSpec((None, width, hidden), lambda e, i: (e, 0, 0)),
            pl.BlockSpec((None, hidden, width), lambda e, i: (e, 0, 0)),
        ],
        out_specs=[
            pl.BlockSpec((2, None, ROW_TILE, width), lambda e, i: (0, e, i, 0)),
            pl.BlockSpec((None, ROW_TILE, hidden), lambda e, i: (e, i, 0)),
            pl.BlockSpec((None, ROW_TILE, hidden), lambda e, i: (e, i, 0)),
        ],
        out_shape=[
            jax.ShapeDtypeStruct((2, experts, rows, width), jnp.bfloat16),
            jax.ShapeDtypeStruct((experts, rows, hidden), jnp.bfloat16),
            jax.ShapeDtypeStruct((experts, rows, hidden), jnp.bfloat16),
        ],
    )(gathered, gathered, w_in_cols, w_out)


def layer_norm(values, gain):
    centred = values - jnp.mean(values, axis=-1, keepdims=True)
    inverse = lax.rsqrt(jnp.mean(centred * centred, axis=-1, keepdims=True) + EPS)
    normed = centred * inverse
    return (normed, inverse, (normed * gain).astype(jnp.bfloat16))


def layer_norm_back(grad_out, normed, inverse, gain):
    scaled = grad_out * gain
    grad_in = inverse * (
        scaled
        - jnp.mean(scaled, axis=-1, keepdims=True)
        - normed * jnp.mean(scaled * normed, axis=-1, keepdims=True)
    )
    return (grad_in, jnp.sum(grad_out * normed, axis=0))


def butterfly_sum(value, axis, size, wire=None):
    step = 1
    while step < size:
        pairs = [(i, i ^ step) for i in range(size)]
        sent = value if wire is None else value.astype(wire)
        other = lax.ppermute(sent, axis, pairs)
        value = sent.astype(jnp.float32) + other.astype(jnp.float32)
        step *= 2
    return value


def heads_view(block, images):
    return block.reshape(images, SEQ, HEADS, HD)


def attention_scores(qkv, images):
    width = HEADS * HD
    query = heads_view(qkv[:, :width], images)
    keys = heads_view(qkv[:, width : 2 * width], images)
    values = heads_view(qkv[:, 2 * width :], images)
    scores = jnp.einsum(
        "bqhd,bkhd->bhqk", query, keys, preferred_element_type=jnp.float32
    ) * HD ** (-0.5)
    return (query, keys, values, scores)


def attention_forward(qkv, images):
    query, keys, values, scores = attention_scores(qkv, images)
    logsum = jax.nn.logsumexp(scores, axis=-1, keepdims=True)
    probs = jnp.exp(scores - logsum).astype(jnp.bfloat16)
    mixed = jnp.einsum("bhqk,bkhd->bqhd", probs, values, preferred_element_type=jnp.float32).astype(
        jnp.bfloat16
    )
    return (mixed.reshape(images * SEQ, HEADS * HD), logsum)


def attention_backward(qkv, mixed, logsum, grad_mixed, images):
    query, keys, values, scores = attention_scores(qkv, images)
    probs_full = jnp.exp(scores - logsum)
    probs = probs_full.astype(jnp.bfloat16)
    grad_out = heads_view(grad_mixed, images)
    out_rows = heads_view(mixed, images)
    grad_values = jnp.einsum("bhqk,bqhd->bkhd", probs, grad_out, preferred_element_type=jnp.float32)
    grad_probs = jnp.einsum("bqhd,bkhd->bhqk", grad_out, values, preferred_element_type=jnp.float32)
    delta = jnp.sum(grad_out.astype(jnp.float32) * out_rows.astype(jnp.float32), axis=-1)
    delta = jnp.transpose(delta, (0, 2, 1))[..., None]
    grad_scores = (probs_full * (grad_probs - delta)).astype(jnp.bfloat16)
    scale = HD ** (-0.5)
    grad_query = (
        jnp.einsum("bhqk,bkhd->bqhd", grad_scores, keys, preferred_element_type=jnp.float32) * scale
    )
    grad_keys = (
        jnp.einsum("bhqk,bqhd->bkhd", grad_scores, query, preferred_element_type=jnp.float32)
        * scale
    )
    width = HEADS * HD
    rows = images * SEQ
    return jnp.concatenate(
        [
            grad_query.reshape(rows, width),
            grad_keys.reshape(rows, width),
            grad_values.reshape(rows, width),
        ],
        axis=1,
    ).astype(jnp.bfloat16)


def route_masks(expert_ids, capacity):
    count = expert_ids.shape[0]
    picked_hot = (expert_ids[:, :, None] == jnp.arange(E_WIN)[None, None, :]).astype(jnp.int32)
    ordered = jnp.transpose(picked_hot, (1, 0, 2)).reshape(2 * count, E_WIN)
    before = jnp.cumsum(ordered, axis=0) - ordered
    position = jnp.sum(before * ordered, axis=1).reshape(2, count).T
    limit = jnp.sum(picked_hot * capacity[None, None, :], axis=2)
    kept_mask = (position < limit).astype(jnp.float32)
    slot_hot = (position[:, :, None] == jnp.arange(CAP)[None, None, :]).astype(jnp.float32)
    return (
        kept_mask[:, :, None, None]
        * picked_hot.astype(jnp.float32)[:, :, :, None]
        * slot_hot[:, :, None, :]
    )


def body(
    inputs,
    norm1_gain,
    w_qkv,
    w_proj,
    norm2_gain,
    w_router,
    w_expert_in,
    w_expert_out,
    expert_ids,
    capacity,
    cotangent,
):
    high = lax.Precision.HIGHEST
    images = inputs.shape[0] // SEQ
    shard_rows = w_qkv.shape[0]
    hid_rows = w_expert_out.shape[1]
    width = HEADS * HD
    dense_all = lax.all_gather(
        jnp.concatenate([w_qkv, w_proj, w_router], axis=1), "shard", axis=0, tiled=True
    )
    full_qkv, full_proj, full_router = (
        dense_all[:, : 3 * width],
        dense_all[:, 3 * width : 4 * width],
        dense_all[:, 4 * width :],
    )
    x_float = inputs.astype(jnp.float32)
    normed1, inverse1, hidden1 = layer_norm(x_float, norm1_gain)
    qkv = jnp.dot(hidden1, full_qkv, preferred_element_type=jnp.float32).astype(jnp.bfloat16)
    mixed, logsum = attention_forward(qkv, images)
    attended = x_float + jnp.dot(mixed, full_proj, preferred_element_type=jnp.float32)
    normed2, inverse2, hidden2 = layer_norm(attended, norm2_gain)
    logits = jnp.dot(hidden2, full_router, preferred_element_type=jnp.float32)
    router = jax.nn.softmax(logits, axis=-1)
    expert_hot = (expert_ids[:, :, None] == jnp.arange(EXPERTS)[None, None, :]).astype(jnp.float32)
    gate = jnp.sum(router[:, None, :] * expert_hot, axis=2)
    masks = route_masks(expert_ids, capacity)
    dispatch_float = jnp.sum(masks, axis=1)
    dispatch = dispatch_float.astype(jnp.bfloat16)
    combine = jnp.sum(masks * gate[:, :, None, None], axis=1)
    expert_rows = jnp.einsum(
        "rec,rd->ecd", dispatch, hidden2, preferred_element_type=jnp.float32
    ).astype(jnp.bfloat16)
    w_in_cols = lax.all_to_all(w_expert_in, "shard", 2, 1, tiled=True)
    grad = cotangent.astype(jnp.float32)
    grad_eout = jnp.einsum("rec,rd->ecd", combine, grad, precision=high).astype(jnp.bfloat16)
    gathered = lax.all_gather(
        jnp.stack([expert_rows, grad_eout]), "shard", axis=2, tiled=True
    )
    rows_all, geout_all = gathered[0], gathered[1]
    parts, activated, grad_pre = expert_block(gathered, w_in_cols, w_expert_out)
    scattered = lax.psum_scatter(parts, "shard", scatter_dimension=2, tiled=True)
    expert_out, grad_rows = scattered[0], scattered[1]
    eout_float = expert_out.astype(jnp.float32)
    moe = jnp.einsum("rec,ecd->rd", combine, eout_float, precision=high)
    outputs = (attended + moe).astype(jnp.bfloat16)
    matched = jnp.einsum("rd,ecd->rec", grad, eout_float, precision=high)
    grad_gate = jnp.sum(masks * matched[:, None, :, :], axis=(2, 3))
    back_qkv, back_proj, back_router = (full_qkv, full_proj, full_router)
    gin_cols = jnp.einsum("erd,erh->edh", rows_all, grad_pre, preferred_element_type=jnp.float32)
    gin_local = lax.all_to_all(gin_cols.astype(jnp.bfloat16), "shard", 1, 2, tiled=True)
    gout_local = jnp.einsum(
        "erh,erd->ehd", activated, geout_all, preferred_element_type=jnp.float32
    ).astype(jnp.bfloat16)
    grad_probs = jnp.sum(grad_gate[:, :, None] * expert_hot, axis=1)
    grad_logits = (
        router * (grad_probs - jnp.sum(router * grad_probs, axis=-1, keepdims=True))
    ).astype(jnp.bfloat16)
    grad_hidden2 = jnp.einsum(
        "rec,ecd->rd", dispatch, grad_rows, preferred_element_type=jnp.float32
    ) + jnp.einsum("re,de->rd", grad_logits, back_router, preferred_element_type=jnp.float32)
    grad_norm2, gain2 = layer_norm_back(grad_hidden2, normed2, inverse2, norm2_gain)
    grad_attended = grad + grad_norm2
    grad_branch = grad_attended.astype(jnp.bfloat16)
    grad_mixed = jnp.einsum(
        "rk,dk->rd", grad_branch, back_proj, preferred_element_type=jnp.float32
    ).astype(jnp.bfloat16)
    grad_qkv_rows = attention_backward(qkv, mixed, logsum, grad_mixed, images)
    grad_hidden1 = jnp.einsum(
        "rk,dk->rd", grad_qkv_rows, back_qkv, preferred_element_type=jnp.float32
    )
    grad_norm1, gain1 = layer_norm_back(grad_hidden1, normed1, inverse1, norm1_gain)
    grad_inputs = grad_attended + grad_norm1
    n_shard = lax.axis_size("shard")
    n_rep = lax.axis_size("rep")
    gains = butterfly_sum(jnp.stack([gain1, gain2]), "shard", n_shard)
    gains = butterfly_sum(gains, "rep", n_rep)
    gain1_total, gain2_total = gains[0], gains[1]
    dense_local = lax.psum_scatter(
        jnp.concatenate(
            [
                jnp.einsum("rc,rk->ck", hidden1, grad_qkv_rows, preferred_element_type=jnp.float32),
                jnp.einsum("rc,rk->ck", mixed, grad_branch, preferred_element_type=jnp.float32),
                jnp.einsum("rc,rk->ck", hidden2, grad_logits, preferred_element_type=jnp.float32),
            ],
            axis=1,
        ).astype(jnp.bfloat16),
        "shard",
        scatter_dimension=0,
        tiled=True,
    )
    dense_total, in_total, out_total = (
        butterfly_sum(dense_local, "rep", n_rep, jnp.bfloat16),
        butterfly_sum(gin_local, "rep", n_rep, jnp.bfloat16),
        butterfly_sum(gout_local, "rep", n_rep, jnp.bfloat16),
    )
    return (
        outputs,
        grad_inputs,
        gain1_total,
        dense_total[:, : 3 * width],
        dense_total[:, 3 * width : 4 * width],
        gain2_total,
        dense_total[:, 4 * width :],
        in_total,
        out_total,
    )


def solution(mesh):
    in_specs = (
        P(("shard", "rep"), None),
        P(),
        P("shard", None),
        P("shard", None),
        P(),
        P("shard", None),
        P(None, "shard", None),
        P(None, "shard", None),
        P(("shard", "rep"), None),
        P(),
        P(("shard", "rep"), None),
    )
    out_specs = (
        P(("shard", "rep"), None),
        P(("shard", "rep"), None),
        P(),
        P("shard", None),
        P("shard", None),
        P(),
        P("shard", None),
        P(None, "shard", None),
        P(None, "shard", None),
    )
    return jax.shard_map(body, mesh=mesh, in_specs=in_specs, out_specs=out_specs, check_vma=False)
```

```python
import jax
import jax.numpy as jnp
from jax import lax
from jax.experimental import pallas as pl
from jax.sharding import PartitionSpec as P

HEADS = 12
HD = 64
EXPERTS = 32
E_WIN = 2
SEQ = 197
CAP = 128


EPS = 1e-06
ROW_TILE = 256

def expert_kernel(rows_ref, geout_ref, w_in_ref, w_out_ref, parts_ref, act_ref, gpre_ref):
    rows = rows_ref[...]
    w_in = w_in_ref[...]
    w_out = w_out_ref[...]
    pre = jnp.dot(rows, w_in, preferred_element_type=jnp.float32)
    erf_term = lax.erf(pre * 0.7071067811865476)
    activated = (0.5 * pre * (1.0 + erf_term)).astype(jnp.bfloat16)
    act_ref[...] = activated
    parts_ref[0] = jnp.dot(activated, w_out, preferred_element_type=jnp.float32).astype(jnp.bfloat16)
    grad_act = lax.dot_general(
        geout_ref[...], w_out, (((1,), (1,)), ((), ())), preferred_element_type=jnp.float32
    )
    slope = 0.5 * (1.0 + erf_term) + pre * jnp.exp(-0.5 * pre * pre) * 0.3989422804014327
    grad_pre = (grad_act * slope).astype(jnp.bfloat16)
    gpre_ref[...] = grad_pre
    parts_ref[1] = lax.dot_general(
        grad_pre, w_in, (((1,), (1,)), ((), ())), preferred_element_type=jnp.float32
    ).astype(jnp.bfloat16)

def expert_block(gathered, w_in_cols, w_out):
    _, experts, rows, width = gathered.shape
    hidden = w_in_cols.shape[2]
    grid = (experts, rows // ROW_TILE)
    return pl.pallas_call(
        expert_kernel,
        grid=grid,
        in_specs=[
            pl.BlockSpec((None, None, ROW_TILE, width), lambda e, i: (0, e, i, 0)),
            pl.BlockSpec((None, None, ROW_TILE, width), lambda e, i: (1, e, i, 0)),
            pl.BlockSpec((None, width, hidden), lambda e, i: (e, 0, 0)),
            pl.BlockSpec((None, hidden, width), lambda e, i: (e, 0, 0)),
        ],
        out_specs=[
            pl.BlockSpec((2, None, ROW_TILE, width), lambda e, i: (0, e, i, 0)),
            pl.BlockSpec((None, ROW_TILE, hidden), lambda e, i: (e, i, 0)),
            pl.BlockSpec((None, ROW_TILE, hidden), lambda e, i: (e, i, 0)),
        ],
        out_shape=[
            jax.ShapeDtypeStruct((2, experts, rows, width), jnp.bfloat16),
            jax.ShapeDtypeStruct((experts, rows, hidden), jnp.bfloat16),
            jax.ShapeDtypeStruct((experts, rows, hidden), jnp.bfloat16),
        ],
    )(gathered, gathered, w_in_cols, w_out)


def layer_norm(values, gain):
    centred = values - jnp.mean(values, axis=-1, keepdims=True)
    inverse = lax.rsqrt(jnp.mean(centred * centred, axis=-1, keepdims=True) + EPS)
    normed = centred * inverse
    return (normed, inverse, (normed * gain).astype(jnp.bfloat16))


def layer_norm_back(grad_out, normed, inverse, gain):
    scaled = grad_out * gain
    grad_in = inverse * (
        scaled
        - jnp.mean(scaled, axis=-1, keepdims=True)
        - normed * jnp.mean(scaled * normed, axis=-1, keepdims=True)
    )
    return (grad_in, jnp.sum(grad_out * normed, axis=0))


def butterfly_sum(value, axis, size, wire=None, radix=2):
    step = 1
    while step < size:
        width = radix if (size // step) % radix == 0 else 2
        sent = value if wire is None else value.astype(wire)
        got = [
            lax.ppermute(sent, axis, [(i, i ^ (shift * step)) for i in range(size)]).astype(jnp.float32)
            for shift in range(1, width)
        ]
        value = sent.astype(jnp.float32) + got[0]
        if width == 4:
            value = value + (got[1] + got[2])
        step *= width
    return value


def heads_view(block, images):
    return block.reshape(images, SEQ, HEADS, HD)


def attention_scores(qkv, images):
    width = HEADS * HD
    query = heads_view(qkv[:, :width], images)
    keys = heads_view(qkv[:, width : 2 * width], images)
    values = heads_view(qkv[:, 2 * width :], images)
    scores = jnp.einsum(
        "bqhd,bkhd->bhqk", query, keys, preferred_element_type=jnp.float32
    ) * HD ** (-0.5)
    return (query, keys, values, scores)


def attention_forward(qkv, images):
    query, keys, values, scores = attention_scores(qkv, images)
    logsum = jax.nn.logsumexp(scores, axis=-1, keepdims=True)
    probs = jnp.exp(scores - logsum).astype(jnp.bfloat16)
    mixed = jnp.einsum("bhqk,bkhd->bqhd", probs, values, preferred_element_type=jnp.float32).astype(
        jnp.bfloat16
    )
    return (mixed.reshape(images * SEQ, HEADS * HD), logsum)


def attention_backward(qkv, mixed, logsum, grad_mixed, images):
    query, keys, values, scores = attention_scores(qkv, images)
    probs_full = jnp.exp(scores - logsum)
    probs = probs_full.astype(jnp.bfloat16)
    grad_out = heads_view(grad_mixed, images)
    out_rows = heads_view(mixed, images)
    grad_values = jnp.einsum("bhqk,bqhd->bkhd", probs, grad_out, preferred_element_type=jnp.float32)
    grad_probs = jnp.einsum("bqhd,bkhd->bhqk", grad_out, values, preferred_element_type=jnp.float32)
    delta = jnp.sum(grad_out.astype(jnp.float32) * out_rows.astype(jnp.float32), axis=-1)
    delta = jnp.transpose(delta, (0, 2, 1))[..., None]
    grad_scores = (probs_full * (grad_probs - delta)).astype(jnp.bfloat16)
    scale = HD ** (-0.5)
    grad_query = (
        jnp.einsum("bhqk,bkhd->bqhd", grad_scores, keys, preferred_element_type=jnp.float32) * scale
    )
    grad_keys = (
        jnp.einsum("bhqk,bqhd->bkhd", grad_scores, query, preferred_element_type=jnp.float32)
        * scale
    )
    width = HEADS * HD
    rows = images * SEQ
    return jnp.concatenate(
        [
            grad_query.reshape(rows, width),
            grad_keys.reshape(rows, width),
            grad_values.reshape(rows, width),
        ],
        axis=1,
    ).astype(jnp.bfloat16)


def route_masks(expert_ids, capacity):
    count = expert_ids.shape[0]
    picked_hot = (expert_ids[:, :, None] == jnp.arange(E_WIN)[None, None, :]).astype(jnp.int32)
    ordered = jnp.transpose(picked_hot, (1, 0, 2)).reshape(2 * count, E_WIN)
    before = jnp.cumsum(ordered, axis=0) - ordered
    position = jnp.sum(before * ordered, axis=1).reshape(2, count).T
    limit = jnp.sum(picked_hot * capacity[None, None, :], axis=2)
    kept_mask = (position < limit).astype(jnp.float32)
    slot_hot = (position[:, :, None] == jnp.arange(CAP)[None, None, :]).astype(jnp.float32)
    return (
        kept_mask[:, :, None, None]
        * picked_hot.astype(jnp.float32)[:, :, :, None]
        * slot_hot[:, :, None, :]
    )


def body(
    inputs,
    norm1_gain,
    w_qkv,
    w_proj,
    norm2_gain,
    w_router,
    w_expert_in,
    w_expert_out,
    expert_ids,
    capacity,
    cotangent,
):
    high = lax.Precision.HIGHEST
    images = inputs.shape[0] // SEQ
    shard_rows = w_qkv.shape[0]
    hid_rows = w_expert_out.shape[1]
    width = HEADS * HD
    dense_all = lax.all_gather(
        jnp.concatenate([w_qkv, w_proj, w_router], axis=1), "shard", axis=0, tiled=True
    )
    full_qkv, full_proj, full_router = (
        dense_all[:, : 3 * width],
        dense_all[:, 3 * width : 4 * width],
        dense_all[:, 4 * width :],
    )
    x_float = inputs.astype(jnp.float32)
    normed1, inverse1, hidden1 = layer_norm(x_float, norm1_gain)
    qkv = jnp.dot(hidden1, full_qkv, preferred_element_type=jnp.float32).astype(jnp.bfloat16)
    mixed, logsum = attention_forward(qkv, images)
    attended = x_float + jnp.dot(mixed, full_proj, preferred_element_type=jnp.float32)
    normed2, inverse2, hidden2 = layer_norm(attended, norm2_gain)
    logits = jnp.dot(hidden2, full_router, preferred_element_type=jnp.float32)
    router = jax.nn.softmax(logits, axis=-1)
    expert_hot = (expert_ids[:, :, None] == jnp.arange(EXPERTS)[None, None, :]).astype(jnp.float32)
    gate = jnp.sum(router[:, None, :] * expert_hot, axis=2)
    masks = route_masks(expert_ids, capacity)
    dispatch_float = jnp.sum(masks, axis=1)
    dispatch = dispatch_float.astype(jnp.bfloat16)
    combine = jnp.sum(masks * gate[:, :, None, None], axis=1)
    expert_rows = jnp.einsum(
        "rec,rd->ecd", dispatch, hidden2, preferred_element_type=jnp.float32
    ).astype(jnp.bfloat16)
    w_in_cols = lax.all_to_all(w_expert_in, "shard", 2, 1, tiled=True)
    grad = cotangent.astype(jnp.float32)
    grad_eout = jnp.einsum("rec,rd->ecd", combine, grad, precision=high).astype(jnp.bfloat16)
    gathered = lax.all_gather(
        jnp.stack([expert_rows, grad_eout]), "shard", axis=2, tiled=True
    )
    rows_all, geout_all = gathered[0], gathered[1]
    parts, activated, grad_pre = expert_block(gathered, w_in_cols, w_expert_out)
    scattered = lax.psum_scatter(parts, "shard", scatter_dimension=2, tiled=True)
    expert_out, grad_rows = scattered[0], scattered[1]
    eout_float = expert_out.astype(jnp.float32)
    moe = jnp.einsum("rec,ecd->rd", combine, eout_float, precision=high)
    outputs = (attended + moe).astype(jnp.bfloat16)
    matched = jnp.einsum("rd,ecd->rec", grad, eout_float, precision=high)
    grad_gate = jnp.sum(masks * matched[:, None, :, :], axis=(2, 3))
    back_qkv, back_proj, back_router = (full_qkv, full_proj, full_router)
    gin_cols = jnp.einsum("erd,erh->edh", rows_all, grad_pre, preferred_element_type=jnp.float32)
    gin_local = lax.all_to_all(gin_cols.astype(jnp.bfloat16), "shard", 1, 2, tiled=True)
    gout_local = jnp.einsum(
        "erh,erd->ehd", activated, geout_all, preferred_element_type=jnp.float32
    ).astype(jnp.bfloat16)
    grad_probs = jnp.sum(grad_gate[:, :, None] * expert_hot, axis=1)
    grad_logits = (
        router * (grad_probs - jnp.sum(router * grad_probs, axis=-1, keepdims=True))
    ).astype(jnp.bfloat16)
    grad_hidden2 = jnp.einsum(
        "rec,ecd->rd", dispatch, grad_rows, preferred_element_type=jnp.float32
    ) + jnp.einsum("re,de->rd", grad_logits, back_router, preferred_element_type=jnp.float32)
    grad_norm2, gain2 = layer_norm_back(grad_hidden2, normed2, inverse2, norm2_gain)
    grad_attended = grad + grad_norm2
    grad_branch = grad_attended.astype(jnp.bfloat16)
    grad_mixed = jnp.einsum(
        "rk,dk->rd", grad_branch, back_proj, preferred_element_type=jnp.float32
    ).astype(jnp.bfloat16)
    grad_qkv_rows = attention_backward(qkv, mixed, logsum, grad_mixed, images)
    grad_hidden1 = jnp.einsum(
        "rk,dk->rd", grad_qkv_rows, back_qkv, preferred_element_type=jnp.float32
    )
    grad_norm1, gain1 = layer_norm_back(grad_hidden1, normed1, inverse1, norm1_gain)
    grad_inputs = grad_attended + grad_norm1
    n_shard = lax.axis_size("shard")
    n_rep = lax.axis_size("rep")
    gains = butterfly_sum(jnp.stack([gain1, gain2]), "shard", n_shard, radix=4)
    gains = butterfly_sum(gains, "rep", n_rep, radix=4)
    gain1_total, gain2_total = gains[0], gains[1]
    dense_local = lax.psum_scatter(
        jnp.concatenate(
            [
                jnp.einsum("rc,rk->ck", hidden1, grad_qkv_rows, preferred_element_type=jnp.float32),
                jnp.einsum("rc,rk->ck", mixed, grad_branch, preferred_element_type=jnp.float32),
                jnp.einsum("rc,rk->ck", hidden2, grad_logits, preferred_element_type=jnp.float32),
            ],
            axis=1,
        ).astype(jnp.bfloat16),
        "shard",
        scatter_dimension=0,
        tiled=True,
    )
    dense_total, in_total, out_total = (
        butterfly_sum(dense_local, "rep", n_rep, jnp.bfloat16),
        butterfly_sum(gin_local, "rep", n_rep, jnp.bfloat16),
        butterfly_sum(gout_local, "rep", n_rep, jnp.bfloat16),
    )
    return (
        outputs,
        grad_inputs,
        gain1_total,
        dense_total[:, : 3 * width],
        dense_total[:, 3 * width : 4 * width],
        gain2_total,
        dense_total[:, 4 * width :],
        in_total,
        out_total,
    )


def solution(mesh):
    in_specs = (
        P(("shard", "rep"), None),
        P(),
        P("shard", None),
        P("shard", None),
        P(),
        P("shard", None),
        P(None, "shard", None),
        P(None, "shard", None),
        P(("shard", "rep"), None),
        P(),
        P(("shard", "rep"), None),
    )
    out_specs = (
        P(("shard", "rep"), None),
        P(("shard", "rep"), None),
        P(),
        P("shard", None),
        P("shard", None),
        P(),
        P("shard", None),
        P(None, "shard", None),
        P(None, "shard", None),
    )
    return jax.shard_map(body, mesh=mesh, in_specs=in_specs, out_specs=out_specs, check_vma=False)
```

```python
import jax
import jax.numpy as jnp
from jax import lax
from jax.experimental import pallas as pl
from jax.sharding import PartitionSpec as P

HEADS = 12
HD = 64
EXPERTS = 32
E_WIN = 2
SEQ = 197
CAP = 128


EPS = 1e-06
ROW_TILE = 256

def expert_kernel(rows_ref, geout_ref, w_in_ref, w_out_ref, parts_ref, act_ref, gpre_ref):
    rows = rows_ref[...]
    w_in = w_in_ref[...]
    w_out = w_out_ref[...]
    pre = jnp.dot(rows, w_in, preferred_element_type=jnp.float32)
    erf_term = lax.erf(pre * 0.7071067811865476)
    activated = (0.5 * pre * (1.0 + erf_term)).astype(jnp.bfloat16)
    act_ref[...] = activated
    parts_ref[0] = jnp.dot(activated, w_out, preferred_element_type=jnp.float32).astype(jnp.bfloat16)
    grad_act = lax.dot_general(
        geout_ref[...], w_out, (((1,), (1,)), ((), ())), preferred_element_type=jnp.float32
    )
    slope = 0.5 * (1.0 + erf_term) + pre * jnp.exp(-0.5 * pre * pre) * 0.3989422804014327
    grad_pre = (grad_act * slope).astype(jnp.bfloat16)
    gpre_ref[...] = grad_pre
    parts_ref[1] = lax.dot_general(
        grad_pre, w_in, (((1,), (1,)), ((), ())), preferred_element_type=jnp.float32
    ).astype(jnp.bfloat16)

def expert_block(gathered, w_in_cols, w_out):
    _, experts, rows, width = gathered.shape
    hidden = w_in_cols.shape[2]
    grid = (experts, rows // ROW_TILE)
    return pl.pallas_call(
        expert_kernel,
        grid=grid,
        in_specs=[
            pl.BlockSpec((None, None, ROW_TILE, width), lambda e, i: (0, e, i, 0)),
            pl.BlockSpec((None, None, ROW_TILE, width), lambda e, i: (1, e, i, 0)),
            pl.BlockSpec((None, width, hidden), lambda e, i: (e, 0, 0)),
            pl.BlockSpec((None, hidden, width), lambda e, i: (e, 0, 0)),
        ],
        out_specs=[
            pl.BlockSpec((2, None, ROW_TILE, width), lambda e, i: (0, e, i, 0)),
            pl.BlockSpec((None, ROW_TILE, hidden), lambda e, i: (e, i, 0)),
            pl.BlockSpec((None, ROW_TILE, hidden), lambda e, i: (e, i, 0)),
        ],
        out_shape=[
            jax.ShapeDtypeStruct((2, experts, rows, width), jnp.bfloat16),
            jax.ShapeDtypeStruct((experts, rows, hidden), jnp.bfloat16),
            jax.ShapeDtypeStruct((experts, rows, hidden), jnp.bfloat16),
        ],
    )(gathered, gathered, w_in_cols, w_out)


def layer_norm(values, gain):
    centred = values - jnp.mean(values, axis=-1, keepdims=True)
    inverse = lax.rsqrt(jnp.mean(centred * centred, axis=-1, keepdims=True) + EPS)
    normed = centred * inverse
    return (normed, inverse, (normed * gain).astype(jnp.bfloat16))


def layer_norm_back(grad_out, normed, inverse, gain):
    scaled = grad_out * gain
    grad_in = inverse * (
        scaled
        - jnp.mean(scaled, axis=-1, keepdims=True)
        - normed * jnp.mean(scaled * normed, axis=-1, keepdims=True)
    )
    return (grad_in, jnp.sum(grad_out * normed, axis=0))


def butterfly_sum(value, axis, size, wire=None):
    step = 1
    while step < size:
        pairs = [(i, i ^ step) for i in range(size)]
        sent = value if wire is None else value.astype(wire)
        other = lax.ppermute(sent, axis, pairs)
        value = sent.astype(jnp.float32) + other.astype(jnp.float32)
        step *= 2
    return value


def heads_view(block, images):
    return block.reshape(images, SEQ, HEADS, HD)


def attention_scores(qkv, images):
    width = HEADS * HD
    query = heads_view(qkv[:, :width], images)
    keys = heads_view(qkv[:, width : 2 * width], images)
    values = heads_view(qkv[:, 2 * width :], images)
    scores = jnp.einsum(
        "bqhd,bkhd->bhqk", query, keys, preferred_element_type=jnp.float32
    ) * HD ** (-0.5)
    return (query, keys, values, scores)


def attention_forward(qkv, images):
    query, keys, values, scores = attention_scores(qkv, images)
    logsum = jax.nn.logsumexp(scores, axis=-1, keepdims=True)
    probs = jnp.exp(scores - logsum).astype(jnp.bfloat16)
    mixed = jnp.einsum("bhqk,bkhd->bqhd", probs, values, preferred_element_type=jnp.float32).astype(
        jnp.bfloat16
    )
    return (mixed.reshape(images * SEQ, HEADS * HD), logsum)


def attention_backward(qkv, mixed, logsum, grad_mixed, images):
    query, keys, values, scores = attention_scores(qkv, images)
    probs_full = jnp.exp(scores - logsum)
    probs = probs_full.astype(jnp.bfloat16)
    grad_out = heads_view(grad_mixed, images)
    out_rows = heads_view(mixed, images)
    grad_values = jnp.einsum("bhqk,bqhd->bkhd", probs, grad_out, preferred_element_type=jnp.float32)
    grad_probs = jnp.einsum("bqhd,bkhd->bhqk", grad_out, values, preferred_element_type=jnp.float32)
    delta = jnp.sum(grad_out.astype(jnp.float32) * out_rows.astype(jnp.float32), axis=-1)
    delta = jnp.transpose(delta, (0, 2, 1))[..., None]
    grad_scores = (probs_full * (grad_probs - delta)).astype(jnp.bfloat16)
    scale = HD ** (-0.5)
    grad_query = (
        jnp.einsum("bhqk,bkhd->bqhd", grad_scores, keys, preferred_element_type=jnp.float32) * scale
    )
    grad_keys = (
        jnp.einsum("bhqk,bqhd->bkhd", grad_scores, query, preferred_element_type=jnp.float32)
        * scale
    )
    width = HEADS * HD
    rows = images * SEQ
    return jnp.concatenate(
        [
            grad_query.reshape(rows, width),
            grad_keys.reshape(rows, width),
            grad_values.reshape(rows, width),
        ],
        axis=1,
    ).astype(jnp.bfloat16)


def route_masks(expert_ids, capacity):
    count = expert_ids.shape[0]
    picked_hot = (expert_ids[:, :, None] == jnp.arange(E_WIN)[None, None, :]).astype(jnp.int32)
    ordered = jnp.transpose(picked_hot, (1, 0, 2)).reshape(2 * count, E_WIN)
    before = jnp.cumsum(ordered, axis=0) - ordered
    position = jnp.sum(before * ordered, axis=1).reshape(2, count).T
    limit = jnp.sum(picked_hot * capacity[None, None, :], axis=2)
    kept_mask = (position < limit).astype(jnp.float32)
    slot_hot = (position[:, :, None] == jnp.arange(CAP)[None, None, :]).astype(jnp.float32)
    return (
        kept_mask[:, :, None, None]
        * picked_hot.astype(jnp.float32)[:, :, :, None]
        * slot_hot[:, :, None, :]
    )


def body(
    inputs,
    norm1_gain,
    w_qkv,
    w_proj,
    norm2_gain,
    w_router,
    w_expert_in,
    w_expert_out,
    expert_ids,
    capacity,
    cotangent,
):
    high = lax.Precision.HIGHEST
    images = inputs.shape[0] // SEQ
    shard_rows = w_qkv.shape[0]
    hid_rows = w_expert_out.shape[1]
    width = HEADS * HD
    dense_all = lax.all_gather(
        jnp.concatenate([w_qkv, w_proj, w_router], axis=1), "shard", axis=0, tiled=True
    )
    full_qkv, full_proj, full_router = (
        dense_all[:, : 3 * width],
        dense_all[:, 3 * width : 4 * width],
        dense_all[:, 4 * width :],
    )
    x_float = inputs.astype(jnp.float32)
    normed1, inverse1, hidden1 = layer_norm(x_float, norm1_gain)
    qkv = jnp.dot(hidden1, full_qkv, preferred_element_type=jnp.float32).astype(jnp.bfloat16)
    mixed, logsum = attention_forward(qkv, images)
    attended = x_float + jnp.dot(mixed, full_proj, preferred_element_type=jnp.float32)
    normed2, inverse2, hidden2 = layer_norm(attended, norm2_gain)
    logits = jnp.dot(hidden2, full_router, preferred_element_type=jnp.float32)
    router = jax.nn.softmax(logits, axis=-1)
    expert_hot = (expert_ids[:, :, None] == jnp.arange(EXPERTS)[None, None, :]).astype(jnp.float32)
    gate = jnp.sum(router[:, None, :] * expert_hot, axis=2)
    masks = route_masks(expert_ids, capacity)
    dispatch_float = jnp.sum(masks, axis=1)
    dispatch = dispatch_float.astype(jnp.bfloat16)
    combine = jnp.sum(masks * gate[:, :, None, None], axis=1)
    expert_rows = jnp.einsum(
        "rec,rd->ecd", dispatch, hidden2, preferred_element_type=jnp.float32
    ).astype(jnp.bfloat16)
    w_in_cols = lax.all_to_all(w_expert_in, "shard", 2, 1, tiled=True)
    grad = cotangent.astype(jnp.float32)
    combine_hi = combine.astype(jnp.bfloat16)
    combine_lo = (combine - combine_hi.astype(jnp.float32)).astype(jnp.bfloat16)
    grad_bf = cotangent
    grad_eout = (
        jnp.einsum("rec,rd->ecd", combine_hi, grad_bf, preferred_element_type=jnp.float32)
        + jnp.einsum("rec,rd->ecd", combine_lo, grad_bf, preferred_element_type=jnp.float32)
    ).astype(jnp.bfloat16)
    gathered = lax.all_gather(
        jnp.stack([expert_rows, grad_eout]), "shard", axis=2, tiled=True
    )
    rows_all, geout_all = gathered[0], gathered[1]
    parts, activated, grad_pre = expert_block(gathered, w_in_cols, w_expert_out)
    scattered = lax.psum_scatter(parts, "shard", scatter_dimension=2, tiled=True)
    expert_out, grad_rows = scattered[0], scattered[1]
    moe = jnp.einsum(
        "rec,ecd->rd", combine_hi, expert_out, preferred_element_type=jnp.float32
    ) + jnp.einsum("rec,ecd->rd", combine_lo, expert_out, preferred_element_type=jnp.float32)
    outputs = (attended + moe).astype(jnp.bfloat16)
    matched = jnp.einsum("rd,ecd->rec", grad_bf, expert_out, preferred_element_type=jnp.float32)
    grad_gate = jnp.sum(masks * matched[:, None, :, :], axis=(2, 3))
    back_qkv, back_proj, back_router = (full_qkv, full_proj, full_router)
    gin_cols = jnp.einsum("erd,erh->edh", rows_all, grad_pre, preferred_element_type=jnp.float32)
    gin_local = lax.all_to_all(gin_cols.astype(jnp.bfloat16), "shard", 1, 2, tiled=True)
    gout_local = jnp.einsum(
        "erh,erd->ehd", activated, geout_all, preferred_element_type=jnp.float32
    ).astype(jnp.bfloat16)
    grad_probs = jnp.sum(grad_gate[:, :, None] * expert_hot, axis=1)
    grad_logits = (
        router * (grad_probs - jnp.sum(router * grad_probs, axis=-1, keepdims=True))
    ).astype(jnp.bfloat16)
    grad_hidden2 = jnp.einsum(
        "rec,ecd->rd", dispatch, grad_rows, preferred_element_type=jnp.float32
    ) + jnp.einsum("re,de->rd", grad_logits, back_router, preferred_element_type=jnp.float32)
    grad_norm2, gain2 = layer_norm_back(grad_hidden2, normed2, inverse2, norm2_gain)
    grad_attended = grad + grad_norm2
    grad_branch = grad_attended.astype(jnp.bfloat16)
    grad_mixed = jnp.einsum(
        "rk,dk->rd", grad_branch, back_proj, preferred_element_type=jnp.float32
    ).astype(jnp.bfloat16)
    grad_qkv_rows = attention_backward(qkv, mixed, logsum, grad_mixed, images)
    grad_hidden1 = jnp.einsum(
        "rk,dk->rd", grad_qkv_rows, back_qkv, preferred_element_type=jnp.float32
    )
    grad_norm1, gain1 = layer_norm_back(grad_hidden1, normed1, inverse1, norm1_gain)
    grad_inputs = grad_attended + grad_norm1
    n_shard = lax.axis_size("shard")
    n_rep = lax.axis_size("rep")
    gains = butterfly_sum(jnp.stack([gain1, gain2]), "shard", n_shard)
    gains = butterfly_sum(gains, "rep", n_rep)
    gain1_total, gain2_total = gains[0], gains[1]
    dense_local = lax.psum_scatter(
        jnp.concatenate(
            [
                jnp.einsum("rc,rk->ck", hidden1, grad_qkv_rows, preferred_element_type=jnp.float32),
                jnp.einsum("rc,rk->ck", mixed, grad_branch, preferred_element_type=jnp.float32),
                jnp.einsum("rc,rk->ck", hidden2, grad_logits, preferred_element_type=jnp.float32),
            ],
            axis=1,
        ).astype(jnp.bfloat16),
        "shard",
        scatter_dimension=0,
        tiled=True,
    )
    dense_total, in_total, out_total = (
        butterfly_sum(dense_local, "rep", n_rep, jnp.bfloat16),
        butterfly_sum(gin_local, "rep", n_rep, jnp.bfloat16),
        butterfly_sum(gout_local, "rep", n_rep, jnp.bfloat16),
    )
    return (
        outputs,
        grad_inputs,
        gain1_total,
        dense_total[:, : 3 * width],
        dense_total[:, 3 * width : 4 * width],
        gain2_total,
        dense_total[:, 4 * width :],
        in_total,
        out_total,
    )


def solution(mesh):
    in_specs = (
        P(("shard", "rep"), None),
        P(),
        P("shard", None),
        P("shard", None),
        P(),
        P("shard", None),
        P(None, "shard", None),
        P(None, "shard", None),
        P(("shard", "rep"), None),
        P(),
        P(("shard", "rep"), None),
    )
    out_specs = (
        P(("shard", "rep"), None),
        P(("shard", "rep"), None),
        P(),
        P("shard", None),
        P("shard", None),
        P(),
        P("shard", None),
        P(None, "shard", None),
        P(None, "shard", None),
    )
    return jax.shard_map(body, mesh=mesh, in_specs=in_specs, out_specs=out_specs, check_vma=False)
```
